768 devices in a mesh: ctx: 64 (over x, y, core), inner: 12 (over z).
Axes of the slice: x: 4, y: 8, z: 12, core: 2. Of those that a mesh axis runs over, the one named last changes fastest.
Arguments:
- low_rank: bfloat16 [49152, 32], P(('ctx', 'inner')), may hold values from -6 to 6
- q_base: bfloat16 [49152, 4608], P(('ctx', 'inner')), may hold values from -6 to 6
- k_base: bfloat16 [49152, 4608], P(('ctx', 'inner')), may hold values from -6 to 6
- v_base: bfloat16 [49152, 4608], P(('ctx', 'inner')), may hold values from -6 to 6
- edit_up: bfloat16 [32, 13824], replicated, may hold values from -0.5 to 0.5
- log_decay: bfloat16 [49152, 36], P(('ctx', 'inner')), may hold values from -1 to 0
- lengths: int32 [64], P('ctx'), may hold values from 384 to 768, as said below
- norm_gain: float32 [4608], replicated, may hold values from 0.5 to 1.5
Outputs:
- attended: bfloat16 [49152, 4608], P(('ctx', 'inner'))
The draws below stay inside these ranges and needn't reach their ends.
Inputs may be any that keep to these rules, and one draw needn't show every extreme that they name: `lengths`: every segment keeps at least half of its tokens, and some segment is full.
All inputs are finite; a program needn't handle non-finite values.
Results may differ from the reference program's by a relative error of at most 0.0072.
Values may be sent and summed in bfloat16 or wider, within the bound.
A program may use at most 64 MiB of HBM per device.

```python
import math
import jax
import jax.numpy as jnp
from jax import lax

DECAYING_HEADS = 36
DH = 128
R = 32
SEG_TOK = 768
SEGS = 64
DOCUMENT_TOKENS = 49152
HD = 4608
N_INNER = 12


def segment_gain(key):
    gain_key = jax.random.fold_in(key, 7001)
    phase_key, loud_key, quiet_key = jax.random.split(gain_key, 3)
    loud_span = max(2, min(16, SEGS // 4))
    start_phase = jax.random.randint(phase_key, (), 0, loud_span)
    segment_ids = jnp.arange(SEGS, dtype=jnp.int32)
    loud_flag = ((segment_ids + start_phase) % loud_span == 0) | (segment_ids == SEGS // 2)
    loud_gain = jnp.exp(jax.random.uniform(loud_key, (SEGS,), jnp.float32, jnp.log(0.5), jnp.log(1.0)))
    quiet_gain = jnp.exp(jax.random.uniform(quiet_key, (SEGS,), jnp.float32, jnp.log(0.004), jnp.log(0.012)))
    return jnp.repeat(jnp.where(loud_flag, loud_gain, quiet_gain), SEG_TOK)


def gained_field(key, salt_value, columns):
    field_key = jax.random.fold_in(key, salt_value)
    noise_field = jax.random.truncated_normal(field_key, -6.0, 6.0, (DOCUMENT_TOKENS, columns), jnp.float32)
    return (noise_field * segment_gain(key)[:, None]).astype(jnp.bfloat16)


def draw_low_rank(key, part):
    return gained_field(key, 11, R)


def draw_k_base(key, part):
    return gained_field(key, 12, HD)


def draw_v_base(key, part):
    return gained_field(key, 13, HD)


def draw_log_decay(key, part):
    gathered_keys = jax.random.split(key, 9)
    fast_count = max(1, DECAYING_HEADS // 2)
    slow_low = 0.6
    slow_high = 1.8
    head_order = jax.random.permutation(gathered_keys[0], DECAYING_HEADS)
    rapid_decay_heads = head_order < fast_count
    slow_rate = jnp.exp(jax.random.uniform(gathered_keys[1], (DECAYING_HEADS,), jnp.float32, jnp.log(slow_low), jnp.log(slow_high))) / SEG_TOK
    fast_base = jnp.exp(jax.random.uniform(gathered_keys[2], (DECAYING_HEADS,), jnp.float32, jnp.log(0.1), jnp.log(0.3))) / SEG_TOK
    per_head_decay = jnp.where(rapid_decay_heads, fast_base, slow_rate)
    segment_multiplier = jnp.exp(jax.random.uniform(gathered_keys[3], (SEGS, 1, DECAYING_HEADS), jnp.float32, jnp.log(0.5), jnp.log(2.0)))
    segment_multiplier = jnp.broadcast_to(segment_multiplier, (SEGS, SEG_TOK, DECAYING_HEADS)).reshape(DOCUMENT_TOKENS, DECAYING_HEADS)
    random_offset = jnp.exp(jax.random.uniform(gathered_keys[4], (DOCUMENT_TOKENS, DECAYING_HEADS), jnp.float32, jnp.log(0.5), jnp.log(2.0)))
    gentle_component = -per_head_decay[None, :] * segment_multiplier * random_offset
    sudden_rows = jax.random.uniform(gathered_keys[5], (DOCUMENT_TOKENS, DECAYING_HEADS), jnp.float32) < 1.0 / 40.0
    sudden_magnitude = jax.random.uniform(gathered_keys[6], (DOCUMENT_TOKENS, DECAYING_HEADS), jnp.float32, 0.6, 0.95)
    sudden_component = jnp.where(sudden_rows & rapid_decay_heads[None, :], -sudden_magnitude, 0.0)
    spike_position = jax.random.randint(gathered_keys[7], (3,), 0, DOCUMENT_TOKENS)
    outlier_rows = jnp.any(jnp.arange(DOCUMENT_TOKENS)[:, None] == spike_position[None, :], axis=1)
    outlier_weight = jnp.log(jax.random.uniform(gathered_keys[8], (DOCUMENT_TOKENS, DECAYING_HEADS), jnp.float32, 0.55, 0.8))
    merged_output = gentle_component + sudden_component + jnp.where(outlier_rows[:, None], outlier_weight, 0.0)
    return jnp.clip(merged_output, -1.0, 0.0).astype(jnp.bfloat16)


def draw_lengths(key, part):
    first_key, second_key = jax.random.split(key, 2)
    drawn = jax.random.randint(first_key, (SEGS,), SEG_TOK // 2, SEG_TOK + 1)
    full_one = jax.random.randint(second_key, (), 0, SEGS)
    return jnp.where(jnp.arange(SEGS) == full_one, SEG_TOK, drawn).astype(jnp.int32)


def level_of(rng, dims, cuts, low, largest):
    def one(position, blocks):
        draws = jax.random.uniform(jax.random.fold_in(jax.random.fold_in(rng, 6), position), (blocks,), jnp.float32, low / len(cuts), largest / len(cuts))
        return jnp.repeat(jnp.exp(draws), dims[position] // blocks).reshape((-1,) + (1,) * (len(dims) - position - 1))

    loudness = one(*cuts[0])
    for cut in cuts[1:]:
        loudness = loudness * one(*cut)
    return loudness


def gaussian(rng, dims, spread, limit, cuts=(), kind=jnp.bfloat16):
    values = spread * jax.random.normal(rng, dims, jnp.float32)
    if cuts:
        values = values * level_of(rng, dims, cuts, -0.22, 0.18)
    return jnp.clip(values, -limit, limit).astype(kind)


def setup_inputs(seed: int = 0) -> dict:
    key_list = jax.random.split(jax.random.key(seed), 9)
    low_rank = draw_low_rank(jax.random.fold_in(key_list[8], 71), 0)
    q_base = gaussian(key_list[1], (DOCUMENT_TOKENS, HD), 1.0, 6.0, ((0, 768),))
    k_base = draw_k_base(jax.random.fold_in(key_list[8], 71), 0)
    v_base = draw_v_base(jax.random.fold_in(key_list[8], 71), 0)
    edit_up = gaussian(key_list[4], (R, 3 * HD), (4 * R) ** -0.5, 0.5)
    log_decay = draw_log_decay(jax.random.fold_in(key_list[8], 71), 0)
    lengths = draw_lengths(jax.random.fold_in(key_list[8], 71), 0)
    norm_gain = jnp.clip(1.0 + 0.1 * jax.random.normal(key_list[7], (HD,), jnp.float32), 0.5, 1.5)
    return dict(low_rank=low_rank, q_base=q_base, k_base=k_base, v_base=v_base, edit_up=edit_up, log_decay=log_decay, lengths=lengths, norm_gain=norm_gain)


def rounded(values):
    return lax.optimization_barrier(values.astype(jnp.bfloat16)).astype(jnp.float32)

def reference(low_rank, q_base, k_base, v_base, edit_up, log_decay, lengths, norm_gain):
    full_width = DECAYING_HEADS * DH
    tile_count = math.gcd(N_INNER, max(1, SEG_TOK // 512))
    block_rows = SEG_TOK // tile_count
    order_ids = jnp.arange(block_rows, dtype=jnp.int32)
    causal = (order_ids[:, None] >= order_ids[None, :])[None]

    def segment(carry_state, inputs):
        rank_rows, q_rows, k_rows, v_rows, decay_rows, seg_length = inputs
        edit_term = jnp.dot(rank_rows, edit_up, preferred_element_type=jnp.float32)
        positions = jnp.arange(SEG_TOK, dtype=jnp.int32)
        live_rows = (positions < seg_length)[:, None]
        queries = rounded(q_rows.astype(jnp.float32) + edit_term[:, :full_width])
        keys_all = rounded(jnp.where(live_rows, k_rows.astype(jnp.float32) + edit_term[:, full_width:2 * full_width], 0.0))
        values_all = rounded(jnp.where(live_rows, v_rows.astype(jnp.float32) + edit_term[:, 2 * full_width:], 0.0))
        query_heads = queries.reshape(SEG_TOK, DECAYING_HEADS, DH)
        key_heads = keys_all.reshape(SEG_TOK, DECAYING_HEADS, DH)
        value_heads = values_all.reshape(SEG_TOK, DECAYING_HEADS, DH)
        decay_sum = jnp.cumsum(decay_rows.astype(jnp.float32), axis=0)
        ending = decay_sum[-1]
        scaled = rounded(key_heads * jnp.exp(ending[None, :] - decay_sum)[:, :, None])
        seg_state = jnp.einsum('shd,she->hde', scaled, value_heads)
        sum_heads = decay_sum.T
        pieces = []
        for first in range(tile_count):
            lower = first * block_rows
            query_part = query_heads[lower:lower + block_rows]
            total = jnp.zeros((block_rows, DECAYING_HEADS, DH), jnp.float32)
            for second in range(first + 1):
                start = second * block_rows
                key_part = key_heads[start:start + block_rows]
                value_part = value_heads[start:start + block_rows]
                scores = jnp.einsum('thd,shd->hts', query_part, key_part)
                gap_log = sum_heads[:, lower:lower + block_rows, None] - sum_heads[:, None, start:start + block_rows]
                if second == first:
                    weights = rounded(jnp.where(causal, scores * jnp.exp(jnp.where(causal, gap_log, 0.0)), 0.0))
                else:
                    weights = rounded(scores * jnp.exp(gap_log))
                total = total + jnp.einsum('hts,shd->thd', weights, value_part)
            pieces.append(total)
        intra_term = jnp.concatenate(pieces, axis=0)
        former = rounded(carry_state)
        inter_term = jnp.exp(decay_sum)[:, :, None] * jnp.einsum('thd,hde->the', query_heads, former)
        mixed_out = (intra_term + inter_term).astype(jnp.bfloat16).reshape(SEG_TOK, full_width)
        mixed_out = jnp.where(live_rows, mixed_out, jnp.zeros_like(mixed_out))
        flat_out = mixed_out.astype(jnp.float32)
        inv_rms = lax.rsqrt(lax.optimization_barrier(jnp.mean(flat_out * flat_out, axis=-1, keepdims=True)) + 1e-06)
        attended = (flat_out * inv_rms * norm_gain[None, :]).astype(jnp.bfloat16)
        next_state = jnp.exp(ending)[:, None, None] * carry_state + seg_state
        return (next_state, attended)
    start_state = jnp.zeros((DECAYING_HEADS, DH, DH), jnp.float32)
    inputs = (low_rank.reshape(SEGS, SEG_TOK, R), q_base.reshape(SEGS, SEG_TOK, full_width), k_base.reshape(SEGS, SEG_TOK, full_width), v_base.reshape(SEGS, SEG_TOK, full_width), log_decay.reshape(SEGS, SEG_TOK, DECAYING_HEADS), lengths.astype(jnp.int32))
    final_state, outputs = lax.scan(segment, start_state, inputs)
    return outputs.reshape(DOCUMENT_TOKENS, full_width)
```

```python
import functools

import jax
import jax.numpy as jnp
from jax import lax
from jax.experimental import pallas as pl
from jax.experimental.pallas import tpu as pltpu
from jax.sharding import PartitionSpec as P

MESH = pl.DeviceIdType.MESH
F32 = jnp.float32
BF16 = jnp.bfloat16
GROUP = 16
STRIDE = 3


def across(a, b, left, right):
    return lax.dot_general(a, b, (((left,), (right,)), ((), ())), preferred_element_type=F32)


def kernel(
    sizes,
    lr_ref, q_hbm, k_hbm, v_hbm, up_hbm, ld_ref, gain_ref, len_ref,
    out_ref,
    qv, kv, vv, up, dbc, drow, st, esend, ebuf, cols,
    ms_s, ms_r, ps_s, ps_r, ch_s, ch_r,
    c_s, c_r, pre, cum, f_s, f_r, x_s, x_r, ag, oac, gac,
    in_sem, es_sem, er_sem, rs_sem, rr_sem, chs_sem, chr_sem,
    cs_sem, cr_sem, fs_sem, fr_sem, xs_sem, xr_sem, as_sem, ar_sem,
):
    zn, group, nx, heads, hp, rows, dh = sizes
    nm = zn // 2
    np_ = zn - 1 - nm
    wide = heads * dh
    slab = dh // group
    z = lax.axis_index("inner")
    c = lax.axis_index("ctx")
    r = lax.rem(c, group)
    x = c // group
    up_z = lax.rem(z + 1, zn)
    down_z = lax.rem(z + zn - 1, zn)

    def owner_of(shift):
        return lax.rem(z + shift + zn, zn)

    def send(src, dst, s_sem, r_sem, where):
        copy = pltpu.make_async_remote_copy(
            src_ref=src, dst_ref=dst, send_sem=s_sem, recv_sem=r_sem,
            device_id=where, device_id_type=MESH,
        )
        return copy

    loads = [
        pltpu.make_async_copy(src, dst, in_sem.at[i])
        for i, (src, dst) in enumerate(((k_hbm, kv), (v_hbm, vv), (up_hbm, up), (q_hbm, qv)))
    ]
    for load in loads:
        load.start()

    barrier = pltpu.get_barrier_semaphore()

    def greet_z(i, carry):
        pl.semaphore_signal(
            barrier, inc=1, device_id={"inner": lax.rem(z + i, zn)}, device_id_type=MESH
        )
        return carry

    def greet_r(i, carry):
        pl.semaphore_signal(
            barrier, inc=1, device_id={"ctx": x * group + lax.rem(r + i, group)},
            device_id_type=MESH,
        )
        return carry

    def greet_x(i, carry):
        pl.semaphore_signal(
            barrier, inc=1, device_id={"ctx": lax.rem(x + i, nx) * group + r},
            device_id_type=MESH,
        )
        return carry

    lax.fori_loop(1, zn, greet_z, 0)
    lax.fori_loop(1, group, greet_r, 0)
    lax.fori_loop(1, nx, greet_x, 0)

    ld = ld_ref[...]
    row_i = lax.broadcasted_iota(jnp.int32, (rows, rows), 0)
    col_i = lax.broadcasted_iota(jnp.int32, (rows, rows), 1)
    causal = row_i >= col_i
    tri = causal.astype(F32).astype(BF16)
    triu = (row_i <= col_i).astype(F32).astype(BF16)
    drow[...] = jnp.dot(ld, triu, preferred_element_type=F32)
    lane_head = lax.broadcasted_iota(jnp.int32, (heads, dh), 1)
    pick = (lane_head == lax.broadcasted_iota(jnp.int32, (heads, dh), 0)).astype(F32).astype(BF16)
    per_head = across(ld, pick, 0, 0).astype(BF16)
    esend[...] = jnp.dot(jnp.ones((8, rows), BF16), per_head, preferred_element_type=F32)[0:1]
    ebuf[z] = esend[...]

    pl.semaphore_wait(barrier, (zn - 1) + (group - 1) + (nx - 1))

    def send_e(i, carry):
        to = lax.rem(z + i, zn)
        send(esend, ebuf.at[z], es_sem.at[i], er_sem.at[z], {"inner": to}).start()
        return carry

    lax.fori_loop(1, zn, send_e, 0)

    def decay_cols(o, carry):
        lane = lax.broadcasted_iota(jnp.int32, (heads, hp * dh), 1)
        head = lax.broadcasted_iota(jnp.int32, (heads, hp * dh), 0)
        low = (head - o * hp) * dh
        sel = ((lane >= low) & (lane < low + dh)).astype(F32).astype(BF16)
        spread = across(ld, sel, 0, 0).astype(BF16)
        at = pl.ds(pl.multiple_of(o * hp * dh, hp * dh), hp * dh)
        dbc[:, at] = jnp.dot(tri, spread, preferred_element_type=F32)
        return carry

    lax.fori_loop(0, zn, decay_cols, 0, unroll=2)

    length = len_ref[0]
    live = (lax.broadcasted_iota(jnp.int32, (rows, 1), 0) + z * rows) < length
    lr = lr_ref[...]
    for load in loads[:3]:
        load.wait()

    def chunk_state(o, carry):
        at = pl.ds(pl.multiple_of(o * hp * dh, hp * dh), hp * dh)
        at_k = pl.ds(pl.multiple_of(wide + o * hp * dh, hp * dh), hp * dh)
        at_v = pl.ds(pl.multiple_of(2 * wide + o * hp * dh, hp * dh), hp * dh)
        kb = jnp.where(live, kv[:, at].astype(F32) + across(lr, up[:, at_k], 0, 0), 0.0)
        vb = jnp.where(live, vv[:, at].astype(F32) + across(lr, up[:, at_v], 0, 0), 0.0)
        kb = kb.astype(BF16)
        vb = vb.astype(BF16)
        kv[:, at] = kb
        vv[:, at] = vb
        d = dbc[:, at]
        scaled = (kb.astype(F32) * jnp.exp(d[rows - 1 :, :] - d)).astype(BF16)
        for k in range(hp):
            span = slice(k * dh, (k + 1) * dh)
            st[o * hp + k] = across(scaled[:, span], vb[:, span], 0, 0)
        return carry

    lax.fori_loop(0, zn, chunk_state, 0, unroll=2)

    loads[3].wait()

    def edit_q(o, carry):
        at = pl.ds(pl.multiple_of(o * hp * dh, hp * dh), hp * dh)
        qv[:, at] = (qv[:, at].astype(F32) + across(lr, up[:, at], 0, 0)).astype(BF16)
        return carry

    lax.fori_loop(0, zn, edit_q, 0, unroll=2)

    @pl.when(z == 0)
    def _():
        ch_r[...] = jnp.zeros_like(ch_r)

    def wait_e(i, carry):
        src = lax.rem(z + i, zn)
        send(esend, ebuf.at[src], es_sem.at[i], er_sem.at[src], {"inner": src}).wait_recv()
        return carry

    lax.fori_loop(1, zn, wait_e, 0)
    before = jnp.zeros((1, dh), F32)
    after = jnp.zeros((1, dh), F32)
    whole = jnp.zeros((1, dh), F32)
    for i in range(zn):
        e_i = ebuf[i]
        before = before + jnp.where(z > i, e_i, 0.0)
        after = after + jnp.where(z < i, e_i, 0.0)
        whole = whole + e_i
    eye = lax.broadcasted_iota(jnp.int32, (dh, dh), 0) == lax.broadcasted_iota(
        jnp.int32, (dh, dh), 1
    )
    for i, vec in enumerate((esend[...], after, before, whole)):
        column = jnp.sum(jnp.where(eye, vec, 0.0), axis=1, keepdims=True)
        cols[i] = jnp.broadcast_to(jnp.exp(column), (dh, dh))

    def factor(kind, head):
        return cols[kind, pl.ds(head, 1), :]

    def chain_head(h):
        @pl.when(z > 0)
        def _():
            send(
                ch_s.at[h], ch_r.at[h], chs_sem.at[h], chr_sem.at[h], {"inner": up_z}
            ).wait_recv()

        prior = ch_r[h]

        @pl.when(z < zn - 1)
        def _():
            ch_s[h] = (prior.astype(F32) * factor(0, h) + st[h]).astype(BF16)
            send(
                ch_s.at[h], ch_r.at[h], chs_sem.at[h], chr_sem.at[h], {"inner": up_z}
            ).start()

        at = pl.ds(pl.multiple_of(h * dh, dh), dh)
        qh = qv[:, at]
        d = dbc[:, at]
        scores = across(qh, kv[:, at], 1, 1)
        gap = d[:, 0:rows] - drow[pl.ds(h, 1), :]
        weights = jnp.where(causal, scores * jnp.exp(jnp.where(causal, gap, 0.0)), 0.0)
        oac[:, at] = jnp.dot(
            weights.astype(BF16), vv[:, at], preferred_element_type=F32
        ) + jnp.exp(d) * jnp.dot(qh, prior, preferred_element_type=F32)

    total_steps = heads + STRIDE * (zn - 1)

    def chain(first, last):
        def step(n, carry):
            h = n - STRIDE * z

            @pl.when((h >= 0) & (h < heads))
            def _():
                chain_head(h)

            return carry

        lax.fori_loop(min(first, total_steps), min(last, total_steps), step, 0)

    def minus_copy(s, k):
        return send(
            ms_s.at[s, k], ms_r.at[s, k], rs_sem.at[s, k], rr_sem.at[s, k], {"inner": down_z}
        )

    def plus_copy(s, k):
        return send(
            ps_s.at[s, k], ps_r.at[s, k], rs_sem.at[nm + s, k], rr_sem.at[nm + s, k],
            {"inner": up_z},
        )

    done = 0
    for s in range(nm):
        o = owner_of(s - nm)
        for k in range(hp):
            h = o * hp + k
            part = st[h] * factor(1, h)
            if s:
                minus_copy(s - 1, k).wait_recv()
                part = part + ms_r[s - 1, k].astype(F32)
            ms_s[s, k] = part.astype(BF16)
            minus_copy(s, k).start()
        if s < np_:
            o = owner_of(np_ - s)
            for k in range(hp):
                h = o * hp + k
                part = st[h] * factor(1, h)
                if s:
                    plus_copy(s - 1, k).wait_recv()
                    part = part + ps_r[s - 1, k].astype(F32)
                ps_s[s, k] = part.astype(BF16)
                plus_copy(s, k).start()
        chain(done, done + 3)
        done += 3

    tile_row = lax.broadcasted_iota(jnp.int32, (slab, dh), 0)
    decay_tile = jnp.zeros((slab, dh), F32)
    for k in range(hp):
        h = z * hp + k
        minus_copy(nm - 1, k).wait_recv()
        plus_copy(np_ - 1, k).wait_recv()
        part = st[h] * factor(1, h) + ms_r[nm - 1, k].astype(F32) + ps_r[np_ - 1, k].astype(F32)
        c_s[:, k] = part.reshape(group, slab, dh)
        decay_tile = jnp.where(tile_row == k, factor(3, h), decay_tile)
    c_s[:, hp] = jnp.broadcast_to(decay_tile[None], (group, slab, dh))

    def c_copy(peer, slot):
        return send(
            c_s.at[peer], c_r.at[slot], cs_sem.at[peer], cr_sem.at[slot],
            {"ctx": x * group + peer},
        )

    def f_copy(peer, slot):
        return send(
            f_s.at[peer], f_r.at[slot], fs_sem.at[peer], fr_sem.at[slot],
            {"ctx": x * group + peer},
        )

    def x_copy(i, peer, slot):
        return send(
            x_s, x_r.at[slot], xs_sem.at[i], xr_sem.at[slot], {"ctx": peer * group + r}
        )

    def start_c(i, carry):
        c_copy(lax.rem(r + i, group), r).start()
        return carry

    def wait_c(i, carry):
        peer = lax.rem(r + i, group)
        c_copy(peer, peer).wait_recv()
        return carry

    lax.fori_loop(1, group, start_c, 0)
    c_r[r] = c_s[r]
    chain(done, done + 12)
    done += 12
    lax.fori_loop(1, group, wait_c, 0)

    carry_state = [jnp.zeros((slab, dh), F32) for _ in range(hp)]
    carry_decay = [jnp.ones((1, dh), F32) for _ in range(hp)]
    for i in range(group):
        tile = c_r[i, hp]
        for k in range(hp):
            here = tile[k : k + 1]
            pre[i, k] = carry_state[k]
            cum[i, k] = jnp.broadcast_to(carry_decay[k], (slab, dh))
            carry_state[k] = here * carry_state[k] + c_r[i, k]
            carry_decay[k] = here * carry_decay[k]
    for k in range(hp):
        x_s[k] = carry_state[k]
        x_s[hp + k] = jnp.broadcast_to(carry_decay[k], (slab, dh))

    def start_x(i, carry):
        x_copy(i, lax.rem(x + i, nx), x).start()
        return carry

    def wait_x(i, carry):
        peer = lax.rem(x + i, nx)
        x_copy(i, peer, peer).wait_recv()
        return carry

    lax.fori_loop(1, nx, start_x, 0)
    x_r[x] = x_s[...]
    chain(done, done + 5)
    done += 5
    lax.fori_loop(1, nx, wait_x, 0)
    for k in range(hp):
        entry = jnp.zeros((slab, dh), F32)
        for i in range(nx):
            entry = jnp.where(x > i, x_r[i, hp + k] * entry + x_r[i, k], entry)
        f_s[:, k] = pre[:, k] + cum[:, k] * entry[None]

    def start_f(i, carry):
        f_copy(lax.rem(r + i, group), r).start()
        return carry

    def wait_f(i, carry):
        peer = lax.rem(r + i, group)
        f_copy(peer, peer).wait_recv()
        return carry

    lax.fori_loop(1, group, start_f, 0)
    f_r[r] = f_s[r]
    chain(done, done + 11)
    done += 11
    lax.fori_loop(1, group, wait_f, 0)
    for k in range(hp):
        ag[z, k] = f_r[:, k].reshape(dh, dh).astype(BF16)

    def ag_minus(s, o, k):
        return send(
            ag.at[o, k], ag.at[o, k], as_sem.at[s, k], ar_sem.at[s, k], {"inner": down_z}
        )

    def ag_plus(s, o, k):
        return send(
            ag.at[o, k], ag.at[o, k], as_sem.at[nm + s, k], ar_sem.at[nm + s, k],
            {"inner": up_z},
        )

    def former_term(o):
        for k in range(hp):
            h = o * hp + k
            at = pl.ds(pl.multiple_of(h * dh, dh), dh)
            inter = jnp.dot(qv[:, at], ag[o, k], preferred_element_type=F32)
            gac[:, at] = jnp.exp(dbc[:, at]) * factor(2, h) * inter

    for k in range(hp):
        ag_minus(0, z, k).start()
        ag_plus(0, z, k).start()
    former_term(z)
    rest = -(-max(total_steps - done, 0) // nm)
    for s in range(nm):
        o_m = owner_of(s + 1)
        o_p = owner_of(-1 - s)
        for k in range(hp):
            ag_minus(s, o_m, k).wait_recv()
            if s + 1 < nm:
                ag_minus(s + 1, o_m, k).start()
        if s < np_:
            for k in range(hp):
                ag_plus(s, o_p, k).wait_recv()
                if s + 1 < np_:
                    ag_plus(s + 1, o_p, k).start()
        former_term(o_m)
        if s < np_:
            former_term(o_p)
        chain(done, done + rest)
        done += rest

    def mix(h, acc):
        at = pl.ds(pl.multiple_of(h * dh, dh), dh)
        mixed = jnp.where(live, oac[:, at] + gac[:, at], 0.0).astype(BF16)
        qv[:, at] = mixed
        wide_mixed = mixed.astype(F32)
        return acc + wide_mixed * wide_mixed

    acc = lax.fori_loop(0, heads, mix, jnp.zeros((rows, dh), F32), unroll=4)
    mean = jnp.sum(acc, axis=1, keepdims=True) / wide
    inv = lax.rsqrt(mean + 1e-6)

    def scale(o, carry):
        at = pl.ds(pl.multiple_of(o * hp * dh, hp * dh), hp * dh)
        out_ref[:, at] = (qv[:, at].astype(F32) * inv * gain_ref[:, at]).astype(BF16)
        return carry

    lax.fori_loop(0, zn, scale, 0, unroll=2)

    def left_e(i, carry):
        to = lax.rem(z + i, zn)
        send(esend, ebuf.at[z], es_sem.at[i], er_sem.at[z], {"inner": to}).wait_send()
        return carry

    lax.fori_loop(1, zn, left_e, 0)
    for s in range(nm):
        for k in range(hp):
            minus_copy(s, k).wait_send()
            ag_minus(s, owner_of(s), k).wait_send()
    for s in range(np_):
        for k in range(hp):
            plus_copy(s, k).wait_send()
            ag_plus(s, owner_of(-s), k).wait_send()

    def left_r(i, carry):
        peer = lax.rem(r + i, group)
        c_copy(peer, r).wait_send()
        f_copy(peer, r).wait_send()
        return carry

    lax.fori_loop(1, group, left_r, 0)

    def left_x(i, carry):
        x_copy(i, lax.rem(x + i, nx), x).wait_send()
        return carry

    lax.fori_loop(1, nx, left_x, 0)

    @pl.when(z < zn - 1)
    def _():
        def left_ch(h, carry):
            send(
                ch_s.at[h], ch_r.at[h], chs_sem.at[h], chr_sem.at[h], {"inner": up_z}
            ).wait_send()
            return carry

        lax.fori_loop(0, heads, left_ch, 0)


def shards(low_rank, q_base, k_base, v_base, edit_up, log_decay, lengths, norm_gain):
    rows, wide = q_base.shape
    rank = low_rank.shape[1]
    heads = log_decay.shape[1]
    dh = wide // heads
    zn = lax.axis_size("inner")
    ctx = lax.axis_size("ctx")
    group = GROUP
    nx = ctx // group
    hp = heads // zn
    nm = zn // 2
    np_ = zn - 1 - nm
    slab = dh // group
    sizes = (zn, group, nx, heads, hp, rows, dh)
    vmem = pl.BlockSpec(memory_space=pltpu.VMEM)
    anywhere = pl.BlockSpec(memory_space=pl.ANY)
    dma = pltpu.SemaphoreType.DMA
    call = pl.pallas_call(
        functools.partial(kernel, sizes),
        out_shape=jax.ShapeDtypeStruct((rows, wide), BF16),
        in_specs=[
            vmem, anywhere, anywhere, anywhere, anywhere, vmem, vmem,
            pl.BlockSpec(memory_space=pltpu.SMEM),
        ],
        out_specs=vmem,
        scratch_shapes=[
            pltpu.VMEM((rows, wide), BF16),
            pltpu.VMEM((rows, wide), BF16),
            pltpu.VMEM((rows, wide), BF16),
            pltpu.VMEM((rank, 3 * wide), BF16),
            pltpu.VMEM((rows, wide), F32),
            pltpu.VMEM((heads, rows), F32),
            pltpu.VMEM((heads, dh, dh), F32),
            pltpu.VMEM((1, dh), F32),
            pltpu.VMEM((zn, 1, dh), F32),
            pltpu.VMEM((4, dh, dh), F32),
            pltpu.VMEM((nm, hp, dh, dh), BF16),
            pltpu.VMEM((nm, hp, dh, dh), BF16),
            pltpu.VMEM((np_, hp, dh, dh), BF16),
            pltpu.VMEM((np_, hp, dh, dh), BF16),
            pltpu.VMEM((heads, dh, dh), BF16),
            pltpu.VMEM((heads, dh, dh), BF16),
            pltpu.VMEM((group, hp + 1, slab, dh), F32),
            pltpu.VMEM((group, hp + 1, slab, dh), F32),
            pltpu.VMEM((group, hp, slab, dh), F32),
            pltpu.VMEM((group, hp, slab, dh), F32),
            pltpu.VMEM((group, hp, slab, dh), F32),
            pltpu.VMEM((group, hp, slab, dh), F32),
            pltpu.VMEM((2 * hp, slab, dh), F32),
            pltpu.VMEM((nx, 2 * hp, slab, dh), F32),
            pltpu.VMEM((zn, hp, dh, dh), BF16),
            pltpu.VMEM((rows, wide), F32),
            pltpu.VMEM((rows, wide), F32),
            dma((4,)),
            dma((zn,)), dma((zn,)),
            dma((nm + np_, hp)), dma((nm + np_, hp)),
            dma((heads,)), dma((heads,)),
            dma((group,)), dma((group,)),
            dma((group,)), dma((group,)),
            dma((nx,)), dma((nx,)),
            dma((nm + np_, hp)), dma((nm + np_, hp)),
        ],
        compiler_params=pltpu.CompilerParams(
            collective_id=0, has_side_effects=True, vmem_limit_bytes=60 * 1024 * 1024
        ),
    )
    return call(
        low_rank.T, q_base, k_base, v_base, edit_up, log_decay.T,
        norm_gain.reshape(1, wide), lengths,
    )


def solution(mesh):
    rows = P(("ctx", "inner"), None)
    return jax.shard_map(
        shards,
        mesh=mesh,
        in_specs=(rows, rows, rows, rows, P(), rows, P("ctx"), P()),
        out_specs=rows,
        check_vma=False,
    )
```

```python
import functools

import jax
import jax.numpy as jnp
from jax import lax
from jax.experimental import pallas as pl
from jax.experimental.pallas import tpu as pltpu
from jax.sharding import PartitionSpec as P

MESH = pl.DeviceIdType.MESH
F32 = jnp.float32
BF16 = jnp.bfloat16
GROUP = 16
STRIDE = 4
EARLY = True
REDUCE_MINUS = 6
GATHER_MINUS = 6
REDUCE_STEPS = (1, 1, 1)
GATHER_STEPS = (1, 2, 1)
UNITS = (8, 11)
C_STEPS = (1, 1, 1, 1)
P_STEPS = 24


def split_of(zn, minus):
    minus = min(max(minus, zn // 2), zn - 2)
    return minus, zn - 1 - minus


def across(a, b, left, right):
    return lax.dot_general(a, b, (((left,), (right,)), ((), ())), preferred_element_type=F32)


def kernel(
    sizes,
    lr_ref, q_hbm, k_hbm, v_hbm, up_hbm, ld_ref, gain_ref, len_ref,
    out_ref,
    qv, kv, vv, up, dbc, drow, st, esend, ebuf, cols,
    ms_s, ms_r, ps_s, ps_r, ch_s, ch_r,
    c_s, c_r, pre, cum, f_s, f_r, x_s, x_r, ag, oac, gac,
    in_sem, es_sem, er_sem, rs_sem, rr_sem, chs_sem, chr_sem,
    cs_sem, cr_sem, fs_sem, fr_sem, xs_sem, xr_sem, as_sem, ar_sem,
):
    zn, group, nx, heads, hp, rows, dh = sizes
    rm, rp = split_of(zn, REDUCE_MINUS)
    am, ap = split_of(zn, GATHER_MINUS)
    wide = heads * dh
    slab = dh // group
    z = lax.axis_index("inner")
    c = lax.axis_index("ctx")
    r = lax.rem(c, group)
    x = c // group
    up_z = lax.rem(z + 1, zn)
    down_z = lax.rem(z + zn - 1, zn)

    def owner_of(shift):
        return lax.rem(z + shift + zn, zn)

    def send(src, dst, s_sem, r_sem, where):
        copy = pltpu.make_async_remote_copy(
            src_ref=src, dst_ref=dst, send_sem=s_sem, recv_sem=r_sem,
            device_id=where, device_id_type=MESH,
        )
        return copy

    loads = [
        pltpu.make_async_copy(src, dst, in_sem.at[i])
        for i, (src, dst) in enumerate(((k_hbm, kv), (v_hbm, vv), (up_hbm, up), (q_hbm, qv)))
    ]
    for load in loads:
        load.start()

    barrier = pltpu.get_barrier_semaphore()

    def greet_z(i, carry):
        pl.semaphore_signal(
            barrier, inc=1, device_id={"inner": lax.rem(z + i, zn)}, device_id_type=MESH
        )
        return carry

    def greet_r(i, carry):
        pl.semaphore_signal(
            barrier, inc=1, device_id={"ctx": x * group + lax.rem(r + i, group)},
            device_id_type=MESH,
        )
        return carry

    def greet_x(i, carry):
        pl.semaphore_signal(
            barrier, inc=1, device_id={"ctx": lax.rem(x + i, nx) * group + r},
            device_id_type=MESH,
        )
        return carry

    lax.fori_loop(1, zn, greet_z, 0)
    lax.fori_loop(1, group, greet_r, 0)
    lax.fori_loop(1, nx, greet_x, 0)

    ld = ld_ref[...]
    row_i = lax.broadcasted_iota(jnp.int32, (rows, rows), 0)
    col_i = lax.broadcasted_iota(jnp.int32, (rows, rows), 1)
    causal = row_i >= col_i
    tri = causal.astype(F32).astype(BF16)
    triu = (row_i <= col_i).astype(F32).astype(BF16)
    drow[...] = jnp.dot(ld, triu, preferred_element_type=F32)
    lane_head = lax.broadcasted_iota(jnp.int32, (heads, dh), 1)
    pick = (lane_head == lax.broadcasted_iota(jnp.int32, (heads, dh), 0)).astype(F32).astype(BF16)
    per_head = across(ld, pick, 0, 0).astype(BF16)
    esend[...] = jnp.dot(jnp.ones((8, rows), BF16), per_head, preferred_element_type=F32)[0:1]
    ebuf[z] = esend[...]
    eye = lax.broadcasted_iota(jnp.int32, (dh, dh), 0) == lax.broadcasted_iota(
        jnp.int32, (dh, dh), 1
    )

    def keep_exp(kind, vec):
        column = jnp.sum(jnp.where(eye, vec, 0.0), axis=1, keepdims=True)
        cols[kind] = jnp.broadcast_to(jnp.exp(column), (dh, dh))

    def factor(kind, head):
        return cols[kind, pl.ds(head, 1), :]

    keep_exp(0, esend[...])

    def decay_cols(o, carry):
        lane = lax.broadcasted_iota(jnp.int32, (heads, hp * dh), 1)
        head = lax.broadcasted_iota(jnp.int32, (heads, hp * dh), 0)
        low = (head - o * hp) * dh
        sel = ((lane >= low) & (lane < low + dh)).astype(F32).astype(BF16)
        spread = across(ld, sel, 0, 0).astype(BF16)
        at = pl.ds(pl.multiple_of(o * hp * dh, hp * dh), hp * dh)
        dbc[:, at] = jnp.dot(tri, spread, preferred_element_type=F32)
        return carry

    lax.fori_loop(0, zn, decay_cols, 0, unroll=2)

    @pl.when(z == 0)
    def _():
        ch_r[...] = jnp.zeros_like(ch_r)

    pl.semaphore_wait(barrier, (zn - 1) + (group - 1) + (nx - 1))

    def send_e(i, carry):
        to = lax.rem(z + i, zn)
        send(esend, ebuf.at[z], es_sem.at[i], er_sem.at[z], {"inner": to}).start()
        return carry

    lax.fori_loop(1, zn, send_e, 0)

    def chain_copy(h):
        return send(ch_s.at[h], ch_r.at[h], chs_sem.at[h], chr_sem.at[h], {"inner": up_z})

    def chain_head(h):
        @pl.when(z > 0)
        def _():
            chain_copy(h).wait_recv()

        @pl.when(z < zn - 1)
        def _():
            ch_s[h] = (ch_r[h].astype(F32) * factor(0, h) + st[h]).astype(BF16)
            chain_copy(h).start()

    total_steps = heads + STRIDE * (zn - 1)

    def paced(work, first, last):
        def step(n, carry):
            h = n - STRIDE * z

            @pl.when((h >= 0) & (h < heads))
            def _():
                work(h)

            return carry

        first, last = min(first, total_steps), min(last, total_steps)
        if last == first + 1:
            step(first, 0)
        elif last > first:
            lax.fori_loop(first, last, step, 0)

    progress = {"chain": 0, "prior": 0}

    def chain(count):
        paced(chain_head, progress["chain"], progress["chain"] + count)
        progress["chain"] += count

    length = len_ref[0]
    live = (lax.broadcasted_iota(jnp.int32, (rows, 1), 0) + z * rows) < length
    lr = lr_ref[...]
    for load in loads[:3]:
        load.wait()

    def chunk_state(o):
        at = pl.ds(pl.multiple_of(o * hp * dh, hp * dh), hp * dh)
        at_k = pl.ds(pl.multiple_of(wide + o * hp * dh, hp * dh), hp * dh)
        at_v = pl.ds(pl.multiple_of(2 * wide + o * hp * dh, hp * dh), hp * dh)
        kb = jnp.where(live, kv[:, at].astype(F32) + across(lr, up[:, at_k], 0, 0), 0.0)
        vb = jnp.where(live, vv[:, at].astype(F32) + across(lr, up[:, at_v], 0, 0), 0.0)
        kb = kb.astype(BF16)
        vb = vb.astype(BF16)
        kv[:, at] = kb
        vv[:, at] = vb
        d = dbc[:, at]
        scaled = (kb.astype(F32) * jnp.exp(d[rows - 1 :, :] - d)).astype(BF16)
        for k in range(hp):
            span = slice(k * dh, (k + 1) * dh)
            st[o * hp + k] = across(scaled[:, span], vb[:, span], 0, 0)

    pair = 2 if zn % 2 == 0 else 1

    def state_pair(i, carry):
        for j in range(pair):
            chunk_state(pair * i + j)
        if EARLY:
            h = i - STRIDE * z

            @pl.when((h >= 0) & (h < heads))
            def _():
                chain_head(h)

        return carry

    lax.fori_loop(0, zn // pair, state_pair, 0)
    if EARLY:
        progress["chain"] = zn // pair

    def wait_e(i, carry):
        src = lax.rem(z + i, zn)
        send(esend, ebuf.at[src], es_sem.at[i], er_sem.at[src], {"inner": src}).wait_recv()
        return carry

    lax.fori_loop(1, zn, wait_e, 0)
    before = jnp.zeros((1, dh), F32)
    after = jnp.zeros((1, dh), F32)
    whole = jnp.zeros((1, dh), F32)
    for i in range(zn):
        e_i = ebuf[i]
        before = before + jnp.where(z > i, e_i, 0.0)
        after = after + jnp.where(z < i, e_i, 0.0)
        whole = whole + e_i
    keep_exp(1, after)

    def minus_copy(s, k):
        return send(
            ms_s.at[s, k], ms_r.at[s, k], rs_sem.at[s, k], rr_sem.at[s, k], {"inner": down_z}
        )

    def plus_copy(s, k):
        return send(
            ps_s.at[s, k], ps_r.at[s, k], rs_sem.at[rm + s, k], rr_sem.at[rm + s, k],
            {"inner": up_z},
        )

    def reduce_step(copy, out, got, s, o, k):
        h = o * hp + k
        part = st[h] * factor(1, h)
        if s:
            copy(s - 1, k).wait_recv()
            part = part + got[s - 1, k].astype(F32)
        out[s, k] = part.astype(BF16)
        copy(s, k).start()

    for s in range(rm):
        for k in range(hp):
            if s < rp:
                reduce_step(plus_copy, ps_s, ps_r, s, owner_of(rp - s), k)
            reduce_step(minus_copy, ms_s, ms_r, s, owner_of(s - rm), k)
            if s == 0 and k < hp - 1:
                plus_copy(s, k).wait_send()
                minus_copy(s, k).wait_send()
            chain(REDUCE_STEPS[k])
        if s == 0:
            keep_exp(2, before)
            keep_exp(3, whole)

    tile_row = lax.broadcasted_iota(jnp.int32, (slab, dh), 0)
    tile = jnp.zeros((slab, dh), F32)
    for k in range(hp):
        fall = factor(3, z * hp + k)
        high = fall.astype(BF16).astype(F32)
        tile = jnp.where(tile_row == k, high, tile)
        tile = jnp.where(tile_row == k + 4, fall - high, tile)
    parts = []
    for k in range(hp):
        h = z * hp + k
        plus_copy(rp - 1, k).wait_recv()
        minus_copy(rm - 1, k).wait_recv()
        part = st[h] * factor(1, h) + ms_r[rm - 1, k].astype(F32) + ps_r[rp - 1, k].astype(F32)
        parts.append(part.reshape(group, slab, dh))
    parts.append(jnp.broadcast_to(tile[None], (group, slab, dh)))
    c_s[...] = jnp.stack(parts, axis=1).reshape(group, (hp + 1) * slab, dh).astype(BF16)

    def c_copy(peer, slot):
        return send(
            c_s.at[peer], c_r.at[slot], cs_sem.at[peer], cr_sem.at[slot],
            {"ctx": x * group + peer},
        )

    def f_copy(peer, slot):
        return send(
            f_s.at[peer], f_r.at[slot], fs_sem.at[peer], fr_sem.at[slot],
            {"ctx": x * group + peer},
        )

    def x_copy(i, peer, slot):
        return send(
            x_s, x_r.at[slot], xs_sem.at[i], xr_sem.at[slot], {"ctx": peer * group + r}
        )

    def start_c(i, carry):
        c_copy(lax.rem(r + i, group), r).start()
        return carry

    def wait_c(i, carry):
        peer = lax.rem(r + i, group)
        c_copy(peer, peer).wait_recv()
        return carry

    def edit_q(o, carry):
        at = pl.ds(pl.multiple_of(o * hp * dh, hp * dh), hp * dh)
        qv[:, at] = (qv[:, at].astype(F32) + across(lr, up[:, at], 0, 0)).astype(BF16)
        return carry

    def intra(h):
        at = pl.ds(pl.multiple_of(h * dh, dh), dh)
        scores = across(qv[:, at], kv[:, at], 1, 1)
        gap = dbc[:, at][:, 0:rows] - drow[pl.ds(h, 1), :]
        weights = jnp.where(causal, scores * jnp.exp(jnp.where(causal, gap, 0.0)), 0.0)
        oac[:, at] = jnp.dot(weights.astype(BF16), vv[:, at], preferred_element_type=F32)

    units = heads // 2

    def fill(first, last):
        base = progress["chain"] - first

        def unit(u, carry):
            intra(2 * u)
            intra(2 * u + 1)
            h = u + base - STRIDE * z

            @pl.when((h >= 0) & (h < heads))
            def _():
                chain_head(h)

            return carry

        first, last = min(first, units), min(last, units)
        lax.fori_loop(first, last, unit, 0)
        progress["chain"] += last - first

    def prior_term(h):
        at = pl.ds(pl.multiple_of(h * dh, dh), dh)
        inter = jnp.dot(qv[:, at], ch_r[h], preferred_element_type=F32)
        oac[:, at] = oac[:, at] + jnp.exp(dbc[:, at]) * inter

    def prior(count):
        last = min(progress["prior"] + count, progress["chain"])
        paced(prior_term, progress["prior"], last)
        progress["prior"] = last

    lax.fori_loop(1, group, start_c, 0)
    c_r[r] = c_s[r]
    loads[3].wait()
    chain(C_STEPS[0])
    lax.fori_loop(0, zn, edit_q, 0, unroll=2)
    chain(C_STEPS[1])
    fill(0, UNITS[0])
    lax.fori_loop(1, group, wait_c, 0)

    carry_state = [jnp.zeros((slab, dh), F32) for _ in range(hp)]
    carry_decay = [jnp.ones((1, dh), F32) for _ in range(hp)]
    for i in range(group):
        got = c_r[i].astype(F32).reshape(hp + 1, slab, dh)
        for k in range(hp):
            here = got[hp, k : k + 1] + got[hp, k + 4 : k + 5]
            pre[i, k] = carry_state[k]
            cum[i, k] = jnp.broadcast_to(carry_decay[k], (slab, dh))
            carry_state[k] = here * carry_state[k] + got[k]
            carry_decay[k] = here * carry_decay[k]
    tile = jnp.zeros((slab, dh), F32)
    for k in range(hp):
        x_s[k] = carry_state[k]
        tile = jnp.where(tile_row == k, carry_decay[k], tile)
    x_s[hp] = tile

    def start_x(i, carry):
        x_copy(i, lax.rem(x + i, nx), x).start()
        return carry

    def wait_x(i, carry):
        peer = lax.rem(x + i, nx)
        x_copy(i, peer, peer).wait_recv()
        return carry

    lax.fori_loop(1, nx, start_x, 0)
    x_r[x] = x_s[...]
    chain(C_STEPS[2])
    fill(UNITS[0], UNITS[1])
    lax.fori_loop(1, nx, wait_x, 0)
    formers = []
    for k in range(hp):
        entry = jnp.zeros((slab, dh), F32)
        for i in range(nx):
            entry = jnp.where(x > i, x_r[i, hp, k : k + 1] * entry + x_r[i, k], entry)
        formers.append(pre[:, k] + cum[:, k] * entry[None])
    formers.append(jnp.zeros((group, slab, dh), F32))
    f_s[...] = jnp.stack(formers, axis=1).reshape(group, (hp + 1) * slab, dh).astype(BF16)

    def start_f(i, carry):
        f_copy(lax.rem(r + i, group), r).start()
        return carry

    def wait_f(i, carry):
        peer = lax.rem(r + i, group)
        f_copy(peer, peer).wait_recv()
        return carry

    lax.fori_loop(1, group, start_f, 0)
    f_r[r] = f_s[r]
    chain(C_STEPS[3])
    fill(UNITS[1], units)
    prior(P_STEPS)
    lax.fori_loop(1, group, wait_f, 0)
    got = f_r[...].astype(F32).reshape(group, hp + 1, slab, dh)
    for k in range(hp):
        ag[z, k] = got[:, k].reshape(dh, dh).astype(BF16)

    def ag_minus(s, o, k):
        return send(
            ag.at[o, k], ag.at[o, k], as_sem.at[s, k], ar_sem.at[s, k], {"inner": down_z}
        )

    def ag_plus(s, o, k):
        return send(
            ag.at[o, k], ag.at[o, k], as_sem.at[am + s, k], ar_sem.at[am + s, k],
            {"inner": up_z},
        )

    def former_term(o):
        for k in range(hp):
            h = o * hp + k
            at = pl.ds(pl.multiple_of(h * dh, dh), dh)
            inter = jnp.dot(qv[:, at], ag[o, k], preferred_element_type=F32)
            gac[:, at] = jnp.exp(dbc[:, at]) * factor(2, h) * inter

    for k in range(hp):
        ag_plus(0, z, k).start()
        ag_minus(0, z, k).start()
        if k < hp - 1:
            ag_plus(0, z, k).wait_send()
            ag_minus(0, z, k).wait_send()
        chain(GATHER_STEPS[k])
    former_term(z)
    rest_p = -(-max(total_steps - progress["prior"], 0) // am)
    final = am - 1
    for s in range(am):
        o_m = owner_of(s + 1)
        o_p = owner_of(-1 - s)
        for k in range(hp):
            if s < ap:
                ag_plus(s, o_p, k).wait_recv()
                if s + 1 < ap:
                    ag_plus(s + 1, o_p, k).start()
            ag_minus(s, o_m, k).wait_recv()
            if s + 1 < am:
                ag_minus(s + 1, o_m, k).start()
            chain(total_steps if s == final and k + 1 == hp else GATHER_STEPS[k])
        if s < ap:
            former_term(o_p)
        former_term(o_m)
        prior(total_steps if s == final else rest_p)

    def mix(h, acc):
        at = pl.ds(pl.multiple_of(h * dh, dh), dh)
        mixed = jnp.where(live, oac[:, at] + gac[:, at], 0.0).astype(BF16)
        qv[:, at] = mixed
        wide_mixed = mixed.astype(F32)
        return acc + wide_mixed * wide_mixed

    acc = lax.fori_loop(0, heads, mix, jnp.zeros((rows, dh), F32), unroll=4)
    mean = jnp.sum(acc, axis=1, keepdims=True) / wide
    inv = lax.rsqrt(mean + 1e-6)

    def scale(h, carry):
        at = pl.ds(pl.multiple_of(h * dh, dh), dh)
        gain = gain_ref[pl.ds(h, 1), :]
        out_ref[:, at] = (qv[:, at].astype(F32) * inv * gain).astype(BF16)
        return carry

    lax.fori_loop(0, heads, scale, 0, unroll=4)

    def left_e(i, carry):
        to = lax.rem(z + i, zn)
        send(esend, ebuf.at[z], es_sem.at[i], er_sem.at[z], {"inner": to}).wait_send()
        return carry

    lax.fori_loop(1, zn, left_e, 0)
    for k in range(hp):
        first = 0 if k == hp - 1 else 1
        for s in range(first, rm):
            minus_copy(s, k).wait_send()
        for s in range(first, rp):
            plus_copy(s, k).wait_send()
        for s in range(first, am):
            ag_minus(s, owner_of(s), k).wait_send()
        for s in range(first, ap):
            ag_plus(s, owner_of(-s), k).wait_send()

    def left_r(i, carry):
        peer = lax.rem(r + i, group)
        c_copy(peer, r).wait_send()
        f_copy(peer, r).wait_send()
        return carry

    lax.fori_loop(1, group, left_r, 0)

    def left_x(i, carry):
        x_copy(i, lax.rem(x + i, nx), x).wait_send()
        return carry

    lax.fori_loop(1, nx, left_x, 0)

    @pl.when(z < zn - 1)
    def _():
        def left_ch(h, carry):
            chain_copy(h).wait_send()
            return carry

        lax.fori_loop(0, heads, left_ch, 0)


def shards(low_rank, q_base, k_base, v_base, edit_up, log_decay, lengths, norm_gain):
    rows, wide = q_base.shape
    rank = low_rank.shape[1]
    heads = log_decay.shape[1]
    dh = wide // heads
    zn = lax.axis_size("inner")
    ctx = lax.axis_size("ctx")
    group = GROUP
    nx = ctx // group
    hp = heads // zn
    rm, rp = split_of(zn, REDUCE_MINUS)
    slab = dh // group
    sizes = (zn, group, nx, heads, hp, rows, dh)
    vmem = pl.BlockSpec(memory_space=pltpu.VMEM)
    anywhere = pl.BlockSpec(memory_space=pl.ANY)
    dma = pltpu.SemaphoreType.DMA
    call = pl.pallas_call(
        functools.partial(kernel, sizes),
        out_shape=jax.ShapeDtypeStruct((rows, wide), BF16),
        in_specs=[
            vmem, anywhere, anywhere, anywhere, anywhere, vmem, vmem,
            pl.BlockSpec(memory_space=pltpu.SMEM),
        ],
        out_specs=vmem,
        scratch_shapes=[
            pltpu.VMEM((rows, wide), BF16),
            pltpu.VMEM((rows, wide), BF16),
            pltpu.VMEM((rows, wide), BF16),
            pltpu.VMEM((rank, 3 * wide), BF16),
            pltpu.VMEM((rows, wide), F32),
            pltpu.VMEM((heads, rows), F32),
            pltpu.VMEM((heads, dh, dh), F32),
            pltpu.VMEM((1, dh), F32),
            pltpu.VMEM((zn, 1, dh), F32),
            pltpu.VMEM((4, dh, dh), F32),
            pltpu.VMEM((rm, hp, dh, dh), BF16),
            pltpu.VMEM((rm, hp, dh, dh), BF16),
            pltpu.VMEM((rp, hp, dh, dh), BF16),
            pltpu.VMEM((rp, hp, dh, dh), BF16),
            pltpu.VMEM((heads, dh, dh), BF16),
            pltpu.VMEM((heads, dh, dh), BF16),
            pltpu.VMEM((group, (hp + 1) * slab, dh), BF16),
            pltpu.VMEM((group, (hp + 1) * slab, dh), BF16),
            pltpu.VMEM((group, hp, slab, dh), F32),
            pltpu.VMEM((group, hp, slab, dh), F32),
            pltpu.VMEM((group, (hp + 1) * slab, dh), BF16),
            pltpu.VMEM((group, (hp + 1) * slab, dh), BF16),
            pltpu.VMEM((hp + 1, slab, dh), F32),
            pltpu.VMEM((nx, hp + 1, slab, dh), F32),
            pltpu.VMEM((zn, hp, dh, dh), BF16),
            pltpu.VMEM((rows, wide), F32),
            pltpu.VMEM((rows, wide), F32),
            dma((4,)),
            dma((zn,)), dma((zn,)),
            dma((zn - 1, hp)), dma((zn - 1, hp)),
            dma((heads,)), dma((heads,)),
            dma((group,)), dma((group,)),
            dma((group,)), dma((group,)),
            dma((nx,)), dma((nx,)),
            dma((zn - 1, hp)), dma((zn - 1, hp)),
        ],
        compiler_params=pltpu.CompilerParams(
            collective_id=0, has_side_effects=True, vmem_limit_bytes=60 * 1024 * 1024
        ),
    )
    return call(
        low_rank.T, q_base, k_base, v_base, edit_up, log_decay.T,
        norm_gain.reshape(heads, dh), lengths,
    )


def solution(mesh):
    rows = P(("ctx", "inner"), None)
    return jax.shard_map(
        shards,
        mesh=mesh,
        in_specs=(rows, rows, rows, rows, P(), rows, P("ctx"), P()),
        out_specs=rows,
        check_vma=False,
    )
```

```python
import functools

import jax
import jax.numpy as jnp
from jax import lax
from jax.experimental import pallas as pl
from jax.experimental.pallas import tpu as pltpu
from jax.sharding import PartitionSpec as P

MESH = pl.DeviceIdType.MESH
F32 = jnp.float32
BF16 = jnp.bfloat16
GROUP = 16
STRIDE = 4
EARLY = True
REDUCE_MINUS = 6
GATHER_MINUS = 6
REDUCE_STEPS = (1, 1, 1)
GATHER_STEPS = (1, 2, 1)
UNITS = (8, 11)
C_STEPS = (1, 1, 1, 1)
P_STEPS = 24


def split_of(zn, minus):
    minus = min(max(minus, zn // 2), zn - 2)
    return minus, zn - 1 - minus


def across(a, b, left, right):
    return lax.dot_general(a, b, (((left,), (right,)), ((), ())), preferred_element_type=F32)


def kernel(
    sizes,
    lr_ref, q_hbm, k_hbm, v_hbm, up_hbm, ld_ref, gain_ref, len_ref,
    out_ref,
    qv, kv, vv, up, dbc, drow, st, esend, ebuf, cols,
    ms_s, ms_r, ps_s, ps_r, ch_s, ch_r,
    c_s, c_r, pre, cum, f_s, f_r, x_s, x_r, ag, oac, gac,
    in_sem, es_sem, er_sem, rs_sem, rr_sem, chs_sem, chr_sem,
    cs_sem, cr_sem, fs_sem, fr_sem, xs_sem, xr_sem, as_sem, ar_sem,
):
    zn, group, nx, heads, hp, rows, dh = sizes
    rm, rp = split_of(zn, REDUCE_MINUS)
    am, ap = split_of(zn, GATHER_MINUS)
    wide = heads * dh
    slab = dh // group
    z = lax.axis_index("inner")
    c = lax.axis_index("ctx")
    r = lax.rem(c, group)
    x = c // group
    up_z = lax.rem(z + 1, zn)
    down_z = lax.rem(z + zn - 1, zn)

    def owner_of(shift):
        return lax.rem(z + shift + zn, zn)

    def send(src, dst, s_sem, r_sem, where):
        copy = pltpu.make_async_remote_copy(
            src_ref=src, dst_ref=dst, send_sem=s_sem, recv_sem=r_sem,
            device_id=where, device_id_type=MESH,
        )
        return copy

    loads = [
        pltpu.make_async_copy(src, dst, in_sem.at[i])
        for i, (src, dst) in enumerate(((k_hbm, kv), (v_hbm, vv), (up_hbm, up), (q_hbm, qv)))
    ]
    for load in loads:
        load.start()

    barrier = pltpu.get_barrier_semaphore()

    def greet_z(i, carry):
        pl.semaphore_signal(
            barrier, inc=1, device_id={"inner": lax.rem(z + i, zn)}, device_id_type=MESH
        )
        return carry

    def greet_r(i, carry):
        pl.semaphore_signal(
            barrier, inc=1, device_id={"ctx": x * group + lax.rem(r + i, group)},
            device_id_type=MESH,
        )
        return carry

    def greet_x(i, carry):
        pl.semaphore_signal(
            barrier, inc=1, device_id={"ctx": lax.rem(x + i, nx) * group + r},
            device_id_type=MESH,
        )
        return carry

    lax.fori_loop(1, zn, greet_z, 0)
    lax.fori_loop(1, group, greet_r, 0)
    lax.fori_loop(1, nx, greet_x, 0)

    ld = ld_ref[...]
    row_i = lax.broadcasted_iota(jnp.int32, (rows, rows), 0)
    col_i = lax.broadcasted_iota(jnp.int32, (rows, rows), 1)
    causal = row_i >= col_i
    tri = causal.astype(F32).astype(BF16)
    triu = (row_i <= col_i).astype(F32).astype(BF16)
    drow[...] = jnp.dot(ld, triu, preferred_element_type=F32)
    lane_head = lax.broadcasted_iota(jnp.int32, (heads, dh), 1)
    pick = (lane_head == lax.broadcasted_iota(jnp.int32, (heads, dh), 0)).astype(F32).astype(BF16)
    per_head = across(ld, pick, 0, 0).astype(BF16)
    esend[...] = jnp.dot(jnp.ones((8, rows), BF16), per_head, preferred_element_type=F32)[0:1]
    ebuf[z] = esend[...]
    eye = lax.broadcasted_iota(jnp.int32, (dh, dh), 0) == lax.broadcasted_iota(
        jnp.int32, (dh, dh), 1
    )

    def keep_exp(kind, vec):
        column = jnp.sum(jnp.where(eye, vec, 0.0), axis=1, keepdims=True)
        cols[kind] = jnp.broadcast_to(jnp.exp(column), (dh, dh))

    def factor(kind, head):
        return cols[kind, pl.ds(head, 1), :]

    keep_exp(0, esend[...])

    def decay_cols(o, carry):
        lane = lax.broadcasted_iota(jnp.int32, (heads, hp * dh), 1)
        head = lax.broadcasted_iota(jnp.int32, (heads, hp * dh), 0)
        low = (head - o * hp) * dh
        sel = ((lane >= low) & (lane < low + dh)).astype(F32).astype(BF16)
        spread = across(ld, sel, 0, 0).astype(BF16)
        at = pl.ds(pl.multiple_of(o * hp * dh, hp * dh), hp * dh)
        dbc[:, at] = jnp.dot(tri, spread, preferred_element_type=F32)
        return carry

    lax.fori_loop(0, zn, decay_cols, 0, unroll=2)

    @pl.when(z == 0)
    def _():
        ch_r[...] = jnp.zeros_like(ch_r)

    pl.semaphore_wait(barrier, (zn - 1) + (group - 1) + (nx - 1))

    def send_e(i, carry):
        to = lax.rem(z + i, zn)
        send(esend, ebuf.at[z], es_sem.at[i], er_sem.at[z], {"inner": to}).start()
        return carry

    lax.fori_loop(1, zn, send_e, 0)

    def chain_copy(h):
        return send(ch_s.at[h], ch_r.at[h], chs_sem.at[h], chr_sem.at[h], {"inner": up_z})

    def chain_head(h):
        @pl.when(z > 0)
        def _():
            chain_copy(h).wait_recv()

        @pl.when(z < zn - 1)
        def _():
            ch_s[h] = (ch_r[h].astype(F32) * factor(0, h) + st[h]).astype(BF16)
            chain_copy(h).start()

    total_steps = heads + STRIDE * (zn - 1)

    def paced(work, first, last):
        def step(n, carry):
            h = n - STRIDE * z

            @pl.when((h >= 0) & (h < heads))
            def _():
                work(h)

            return carry

        first, last = min(first, total_steps), min(last, total_steps)
        if last == first + 1:
            step(first, 0)
        elif last > first:
            lax.fori_loop(first, last, step, 0)

    progress = {"chain": 0, "prior": 0}

    def chain(count):
        paced(chain_head, progress["chain"], progress["chain"] + count)
        progress["chain"] += count

    length = len_ref[0]
    live = (lax.broadcasted_iota(jnp.int32, (rows, 1), 0) + z * rows) < length
    lr = lr_ref[...]
    for load in loads[:3]:
        load.wait()

    def chunk_state(o):
        at = pl.ds(pl.multiple_of(o * hp * dh, hp * dh), hp * dh)
        at_k = pl.ds(pl.multiple_of(wide + o * hp * dh, hp * dh), hp * dh)
        at_v = pl.ds(pl.multiple_of(2 * wide + o * hp * dh, hp * dh), hp * dh)
        kb = jnp.where(live, kv[:, at].astype(F32) + across(lr, up[:, at_k], 0, 0), 0.0)
        vb = jnp.where(live, vv[:, at].astype(F32) + across(lr, up[:, at_v], 0, 0), 0.0)
        kb = kb.astype(BF16)
        vb = vb.astype(BF16)
        kv[:, at] = kb
        vv[:, at] = vb
        d = dbc[:, at]
        scaled = (kb.astype(F32) * jnp.exp(d[rows - 1 :, :] - d)).astype(BF16)
        for k in range(hp):
            span = slice(k * dh, (k + 1) * dh)
            st[o * hp + k] = across(scaled[:, span], vb[:, span], 0, 0)

    pair = 2 if zn % 2 == 0 else 1

    def state_pair(i, carry):
        for j in range(pair):
            chunk_state(pair * i + j)
        if EARLY:
            h = i - STRIDE * z

            @pl.when((h >= 0) & (h < heads))
            def _():
                chain_head(h)

        return carry

    lax.fori_loop(0, zn // pair, state_pair, 0)
    if EARLY:
        progress["chain"] = zn // pair

    def wait_e(i, carry):
        src = lax.rem(z + i, zn)
        send(esend, ebuf.at[src], es_sem.at[i], er_sem.at[src], {"inner": src}).wait_recv()
        return carry

    lax.fori_loop(1, zn, wait_e, 0)
    before = jnp.zeros((1, dh), F32)
    after = jnp.zeros((1, dh), F32)
    whole = jnp.zeros((1, dh), F32)
    for i in range(zn):
        e_i = ebuf[i]
        before = before + jnp.where(z > i, e_i, 0.0)
        after = after + jnp.where(z < i, e_i, 0.0)
        whole = whole + e_i
    keep_exp(1, after)

    def minus_copy(s, k):
        return send(
            ms_s.at[s, k], ms_r.at[s, k], rs_sem.at[s, k], rr_sem.at[s, k], {"inner": down_z}
        )

    def plus_copy(s, k):
        return send(
            ps_s.at[s, k], ps_r.at[s, k], rs_sem.at[rm + s, k], rr_sem.at[rm + s, k],
            {"inner": up_z},
        )

    def reduce_step(copy, out, got, s, o, k):
        h = o * hp + k
        part = st[h] * factor(1, h)
        if s:
            copy(s - 1, k).wait_recv()
            part = part + got[s - 1, k].astype(F32)
        out[s, k] = part.astype(BF16)
        copy(s, k).start()

    for s in range(rm):
        for k in range(hp):
            if s < rp:
                reduce_step(plus_copy, ps_s, ps_r, s, owner_of(rp - s), k)
            reduce_step(minus_copy, ms_s, ms_r, s, owner_of(s - rm), k)
            chain(REDUCE_STEPS[k])
        if s == 0:
            keep_exp(2, before)
            keep_exp(3, whole)

    tile_row = lax.broadcasted_iota(jnp.int32, (slab, dh), 0)
    tile = jnp.zeros((slab, dh), F32)
    for k in range(hp):
        fall = factor(3, z * hp + k)
        high = fall.astype(BF16).astype(F32)
        tile = jnp.where(tile_row == k, high, tile)
        tile = jnp.where(tile_row == k + 4, fall - high, tile)
    parts = []
    for k in range(hp):
        h = z * hp + k
        plus_copy(rp - 1, k).wait_recv()
        minus_copy(rm - 1, k).wait_recv()
        part = st[h] * factor(1, h) + ms_r[rm - 1, k].astype(F32) + ps_r[rp - 1, k].astype(F32)
        parts.append(part.reshape(group, slab, dh))
    parts.append(jnp.broadcast_to(tile[None], (group, slab, dh)))
    c_s[...] = jnp.stack(parts, axis=1).reshape(group, (hp + 1) * slab, dh).astype(BF16)

    def c_copy(peer, slot):
        return send(
            c_s.at[peer], c_r.at[slot], cs_sem.at[peer], cr_sem.at[slot],
            {"ctx": x * group + peer},
        )

    def f_copy(peer, slot):
        return send(
            f_s.at[peer], f_r.at[slot], fs_sem.at[peer], fr_sem.at[slot],
            {"ctx": x * group + peer},
        )

    def x_copy(i, peer, slot):
        return send(
            x_s, x_r.at[slot], xs_sem.at[i], xr_sem.at[slot], {"ctx": peer * group + r}
        )

    def start_c(i, carry):
        c_copy(lax.rem(r + i, group), r).start()
        return carry

    def wait_c(i, carry):
        peer = lax.rem(r + i, group)
        c_copy(peer, peer).wait_recv()
        return carry

    def edit_q(o, carry):
        at = pl.ds(pl.multiple_of(o * hp * dh, hp * dh), hp * dh)
        qv[:, at] = (qv[:, at].astype(F32) + across(lr, up[:, at], 0, 0)).astype(BF16)
        return carry

    def intra(h):
        at = pl.ds(pl.multiple_of(h * dh, dh), dh)
        scores = across(qv[:, at], kv[:, at], 1, 1)
        gap = dbc[:, at][:, 0:rows] - drow[pl.ds(h, 1), :]
        weights = jnp.where(causal, scores * jnp.exp(jnp.where(causal, gap, 0.0)), 0.0)
        oac[:, at] = jnp.dot(weights.astype(BF16), vv[:, at], preferred_element_type=F32)

    units = heads // 2

    def fill(first, last):
        base = progress["chain"] - first

        def unit(u, carry):
            intra(2 * u)
            intra(2 * u + 1)
            h = u + base - STRIDE * z

            @pl.when((h >= 0) & (h < heads))
            def _():
                chain_head(h)

            return carry

        first, last = min(first, units), min(last, units)
        lax.fori_loop(first, last, unit, 0)
        progress["chain"] += last - first

    def prior_term(h):
        at = pl.ds(pl.multiple_of(h * dh, dh), dh)
        inter = jnp.dot(qv[:, at], ch_r[h], preferred_element_type=F32)
        oac[:, at] = oac[:, at] + jnp.exp(dbc[:, at]) * inter

    def prior(count):
        last = min(progress["prior"] + count, progress["chain"])
        paced(prior_term, progress["prior"], last)
        progress["prior"] = last

    lax.fori_loop(1, group, start_c, 0)
    c_r[r] = c_s[r]
    loads[3].wait()
    chain(C_STEPS[0])
    lax.fori_loop(0, zn, edit_q, 0, unroll=2)
    chain(C_STEPS[1])
    fill(0, UNITS[0])
    lax.fori_loop(1, group, wait_c, 0)

    carry_state = [jnp.zeros((slab, dh), F32) for _ in range(hp)]
    carry_decay = [jnp.ones((1, dh), F32) for _ in range(hp)]
    for i in range(group):
        got = c_r[i].astype(F32).reshape(hp + 1, slab, dh)
        for k in range(hp):
            here = got[hp, k : k + 1] + got[hp, k + 4 : k + 5]
            pre[i, k] = carry_state[k]
            cum[i, k] = jnp.broadcast_to(carry_decay[k], (slab, dh))
            carry_state[k] = here * carry_state[k] + got[k]
            carry_decay[k] = here * carry_decay[k]
    tile = jnp.zeros((slab, dh), F32)
    for k in range(hp):
        x_s[k] = carry_state[k]
        tile = jnp.where(tile_row == k, carry_decay[k], tile)
    x_s[hp] = tile

    def start_x(i, carry):
        x_copy(i, lax.rem(x + i, nx), x).start()
        return carry

    def wait_x(i, carry):
        peer = lax.rem(x + i, nx)
        x_copy(i, peer, peer).wait_recv()
        return carry

    lax.fori_loop(1, nx, start_x, 0)
    x_r[x] = x_s[...]
    chain(C_STEPS[2])
    fill(UNITS[0], UNITS[1])
    lax.fori_loop(1, nx, wait_x, 0)
    formers = []
    for k in range(hp):
        entry = jnp.zeros((slab, dh), F32)
        for i in range(nx):
            entry = jnp.where(x > i, x_r[i, hp, k : k + 1] * entry + x_r[i, k], entry)
        formers.append(pre[:, k] + cum[:, k] * entry[None])
    formers.append(jnp.zeros((group, slab, dh), F32))
    f_s[...] = jnp.stack(formers, axis=1).reshape(group, (hp + 1) * slab, dh).astype(BF16)

    def start_f(i, carry):
        f_copy(lax.rem(r + i, group), r).start()
        return carry

    def wait_f(i, carry):
        peer = lax.rem(r + i, group)
        f_copy(peer, peer).wait_recv()
        return carry

    lax.fori_loop(1, group, start_f, 0)
    f_r[r] = f_s[r]
    chain(C_STEPS[3])
    fill(UNITS[1], units)
    prior(P_STEPS)
    lax.fori_loop(1, group, wait_f, 0)
    got = f_r[...].astype(F32).reshape(group, hp + 1, slab, dh)
    for k in range(hp):
        ag[z, k] = got[:, k].reshape(dh, dh).astype(BF16)

    def ag_minus(s, o, k):
        return send(
            ag.at[o, k], ag.at[o, k], as_sem.at[s, k], ar_sem.at[s, k], {"inner": down_z}
        )

    def ag_plus(s, o, k):
        return send(
            ag.at[o, k], ag.at[o, k], as_sem.at[am + s, k], ar_sem.at[am + s, k],
            {"inner": up_z},
        )

    def former_term(o):
        for k in range(hp):
            h = o * hp + k
            at = pl.ds(pl.multiple_of(h * dh, dh), dh)
            inter = jnp.dot(qv[:, at], ag[o, k], preferred_element_type=F32)
            gac[:, at] = jnp.exp(dbc[:, at]) * factor(2, h) * inter

    for k in range(hp):
        ag_plus(0, z, k).start()
        ag_minus(0, z, k).start()
        chain(GATHER_STEPS[k])
    former_term(z)
    rest_p = -(-max(total_steps - progress["prior"], 0) // am)
    final = am - 1
    for s in range(am):
        o_m = owner_of(s + 1)
        o_p = owner_of(-1 - s)
        for k in range(hp):
            if s < ap:
                ag_plus(s, o_p, k).wait_recv()
                if s + 1 < ap:
                    ag_plus(s + 1, o_p, k).start()
            ag_minus(s, o_m, k).wait_recv()
            if s + 1 < am:
                ag_minus(s + 1, o_m, k).start()
            chain(total_steps if s == final and k + 1 == hp else GATHER_STEPS[k])
        if s < ap:
            former_term(o_p)
        former_term(o_m)
        prior(total_steps if s == final else rest_p)

    def mix(h, acc):
        at = pl.ds(pl.multiple_of(h * dh, dh), dh)
        mixed = jnp.where(live, oac[:, at] + gac[:, at], 0.0).astype(BF16)
        qv[:, at] = mixed
        wide_mixed = mixed.astype(F32)
        return acc + wide_mixed * wide_mixed

    acc = lax.fori_loop(0, heads, mix, jnp.zeros((rows, dh), F32), unroll=4)
    mean = jnp.sum(acc, axis=1, keepdims=True) / wide
    inv = lax.rsqrt(mean + 1e-6)

    def scale(h, carry):
        at = pl.ds(pl.multiple_of(h * dh, dh), dh)
        gain = gain_ref[pl.ds(h, 1), :]
        out_ref[:, at] = (qv[:, at].astype(F32) * inv * gain).astype(BF16)
        return carry

    lax.fori_loop(0, heads, scale, 0, unroll=4)

    def left_e(i, carry):
        to = lax.rem(z + i, zn)
        send(esend, ebuf.at[z], es_sem.at[i], er_sem.at[z], {"inner": to}).wait_send()
        return carry

    lax.fori_loop(1, zn, left_e, 0)
    for k in range(hp):
        for s in range(rm):
            minus_copy(s, k).wait_send()
        for s in range(rp):
            plus_copy(s, k).wait_send()
        for s in range(am):
            ag_minus(s, owner_of(s), k).wait_send()
        for s in range(ap):
            ag_plus(s, owner_of(-s), k).wait_send()

    def left_r(i, carry):
        peer = lax.rem(r + i, group)
        c_copy(peer, r).wait_send()
        f_copy(peer, r).wait_send()
        return carry

    lax.fori_loop(1, group, left_r, 0)

    def left_x(i, carry):
        x_copy(i, lax.rem(x + i, nx), x).wait_send()
        return carry

    lax.fori_loop(1, nx, left_x, 0)

    @pl.when(z < zn - 1)
    def _():
        def left_ch(h, carry):
            chain_copy(h).wait_send()
            return carry

        lax.fori_loop(0, heads, left_ch, 0)


def shards(low_rank, q_base, k_base, v_base, edit_up, log_decay, lengths, norm_gain):
    rows, wide = q_base.shape
    rank = low_rank.shape[1]
    heads = log_decay.shape[1]
    dh = wide // heads
    zn = lax.axis_size("inner")
    ctx = lax.axis_size("ctx")
    group = GROUP
    nx = ctx // group
    hp = heads // zn
    rm, rp = split_of(zn, REDUCE_MINUS)
    slab = dh // group
    sizes = (zn, group, nx, heads, hp, rows, dh)
    vmem = pl.BlockSpec(memory_space=pltpu.VMEM)
    anywhere = pl.BlockSpec(memory_space=pl.ANY)
    dma = pltpu.SemaphoreType.DMA
    call = pl.pallas_call(
        functools.partial(kernel, sizes),
        out_shape=jax.ShapeDtypeStruct((rows, wide), BF16),
        in_specs=[
            vmem, anywhere, anywhere, anywhere, anywhere, vmem, vmem,
            pl.BlockSpec(memory_space=pltpu.SMEM),
        ],
        out_specs=vmem,
        scratch_shapes=[
            pltpu.VMEM((rows, wide), BF16),
            pltpu.VMEM((rows, wide), BF16),
            pltpu.VMEM((rows, wide), BF16),
            pltpu.VMEM((rank, 3 * wide), BF16),
            pltpu.VMEM((rows, wide), F32),
            pltpu.VMEM((heads, rows), F32),
            pltpu.VMEM((heads, dh, dh), F32),
            pltpu.VMEM((1, dh), F32),
            pltpu.VMEM((zn, 1, dh), F32),
            pltpu.VMEM((4, dh, dh), F32),
            pltpu.VMEM((rm, hp, dh, dh), BF16),
            pltpu.VMEM((rm, hp, dh, dh), BF16),
            pltpu.VMEM((rp, hp, dh, dh), BF16),
            pltpu.VMEM((rp, hp, dh, dh), BF16),
            pltpu.VMEM((heads, dh, dh), BF16),
            pltpu.VMEM((heads, dh, dh), BF16),
            pltpu.VMEM((group, (hp + 1) * slab, dh), BF16),
            pltpu.VMEM((group, (hp + 1) * slab, dh), BF16),
            pltpu.VMEM((group, hp, slab, dh), F32),
            pltpu.VMEM((group, hp, slab, dh), F32),
            pltpu.VMEM((group, (hp + 1) * slab, dh), BF16),
            pltpu.VMEM((group, (hp + 1) * slab, dh), BF16),
            pltpu.VMEM((hp + 1, slab, dh), F32),
            pltpu.VMEM((nx, hp + 1, slab, dh), F32),
            pltpu.VMEM((zn, hp, dh, dh), BF16),
            pltpu.VMEM((rows, wide), F32),
            pltpu.VMEM((rows, wide), F32),
            dma((4,)),
            dma((zn,)), dma((zn,)),
            dma((zn - 1, hp)), dma((zn - 1, hp)),
            dma((heads,)), dma((heads,)),
            dma((group,)), dma((group,)),
            dma((group,)), dma((group,)),
            dma((nx,)), dma((nx,)),
            dma((zn - 1, hp)), dma((zn - 1, hp)),
        ],
        compiler_params=pltpu.CompilerParams(
            collective_id=0, has_side_effects=True, vmem_limit_bytes=60 * 1024 * 1024
        ),
    )
    return call(
        low_rank.T, q_base, k_base, v_base, edit_up, log_decay.T,
        norm_gain.reshape(heads, dh), lengths,
    )


def solution(mesh):
    rows = P(("ctx", "inner"), None)
    return jax.shard_map(
        shards,
        mesh=mesh,
        in_specs=(rows, rows, rows, rows, P(), rows, P("ctx"), P()),
        out_specs=rows,
        check_vma=False,
    )
```

```python
import functools

import jax
import jax.numpy as jnp
from jax import lax
from jax.experimental import pallas as pl
from jax.experimental.pallas import tpu as pltpu
from jax.sharding import PartitionSpec as P

MESH = pl.DeviceIdType.MESH
F32 = jnp.float32
BF16 = jnp.bfloat16
GROUP = 16
STRIDE = 4
EARLY = True
REDUCE_MINUS = 6
GATHER_MINUS = 6
REDUCE_STEPS = (1, 1, 1)
GATHER_STEPS = (1, 2, 1)
UNITS = (8, 11)
C_STEPS = (0, 0, 0, 0)
P_STEPS = 24


def split_of(zn, minus):
    minus = min(max(minus, zn // 2), zn - 2)
    return minus, zn - 1 - minus


def across(a, b, left, right):
    return lax.dot_general(a, b, (((left,), (right,)), ((), ())), preferred_element_type=F32)


def kernel(
    sizes,
    lr_ref, q_hbm, k_hbm, v_hbm, up_hbm, ld_ref, gain_ref, len_ref,
    out_ref,
    qv, kv, vv, up, dbc, drow, st, esend, ebuf, cols,
    ms_s, ms_r, ps_s, ps_r, ch_s, ch_r,
    c_s, c_r, pre, cum, f_s, f_r, x_s, x_r, ag, oac, gac,
    in_sem, es_sem, er_sem, rs_sem, rr_sem, chs_sem, chr_sem,
    cs_sem, cr_sem, fs_sem, fr_sem, xs_sem, xr_sem, as_sem, ar_sem,
):
    zn, group, nx, heads, hp, rows, dh = sizes
    rm, rp = split_of(zn, REDUCE_MINUS)
    am, ap = split_of(zn, GATHER_MINUS)
    wide = heads * dh
    slab = dh // group
    z = lax.axis_index("inner")
    c = lax.axis_index("ctx")
    r = lax.rem(c, group)
    x = c // group
    up_z = lax.rem(z + 1, zn)
    down_z = lax.rem(z + zn - 1, zn)

    def owner_of(shift):
        return lax.rem(z + shift + zn, zn)

    def send(src, dst, s_sem, r_sem, where):
        copy = pltpu.make_async_remote_copy(
            src_ref=src, dst_ref=dst, send_sem=s_sem, recv_sem=r_sem,
            device_id=where, device_id_type=MESH,
        )
        return copy

    loads = [
        pltpu.make_async_copy(src, dst, in_sem.at[i])
        for i, (src, dst) in enumerate(((k_hbm, kv), (v_hbm, vv), (up_hbm, up), (q_hbm, qv)))
    ]
    for load in loads:
        load.start()

    barrier = pltpu.get_barrier_semaphore()

    def greet_z(i, carry):
        pl.semaphore_signal(
            barrier, inc=1, device_id={"inner": lax.rem(z + i, zn)}, device_id_type=MESH
        )
        return carry

    def greet_r(i, carry):
        pl.semaphore_signal(
            barrier, inc=1, device_id={"ctx": x * group + lax.rem(r + i, group)},
            device_id_type=MESH,
        )
        return carry

    def greet_x(i, carry):
        pl.semaphore_signal(
            barrier, inc=1, device_id={"ctx": lax.rem(x + i, nx) * group + r},
            device_id_type=MESH,
        )
        return carry

    lax.fori_loop(1, zn, greet_z, 0)
    lax.fori_loop(1, group, greet_r, 0)
    lax.fori_loop(1, nx, greet_x, 0)

    ld = ld_ref[...]
    row_i = lax.broadcasted_iota(jnp.int32, (rows, rows), 0)
    col_i = lax.broadcasted_iota(jnp.int32, (rows, rows), 1)
    causal = row_i >= col_i
    tri = causal.astype(F32).astype(BF16)
    triu = (row_i <= col_i).astype(F32).astype(BF16)
    drow[...] = jnp.dot(ld, triu, preferred_element_type=F32)
    lane_head = lax.broadcasted_iota(jnp.int32, (heads, dh), 1)
    pick = (lane_head == lax.broadcasted_iota(jnp.int32, (heads, dh), 0)).astype(F32).astype(BF16)
    per_head = across(ld, pick, 0, 0).astype(BF16)
    esend[...] = jnp.dot(jnp.ones((8, rows), BF16), per_head, preferred_element_type=F32)[0:1]
    ebuf[z] = esend[...]
    eye = lax.broadcasted_iota(jnp.int32, (dh, dh), 0) == lax.broadcasted_iota(
        jnp.int32, (dh, dh), 1
    )

    def keep_exp(kind, vec):
        column = jnp.sum(jnp.where(eye, vec, 0.0), axis=1, keepdims=True)
        cols[kind] = jnp.broadcast_to(jnp.exp(column), (dh, dh))

    def factor(kind, head):
        return cols[kind, pl.ds(head, 1), :]

    keep_exp(0, esend[...])

    def decay_cols(o, carry):
        lane = lax.broadcasted_iota(jnp.int32, (heads, hp * dh), 1)
        head = lax.broadcasted_iota(jnp.int32, (heads, hp * dh), 0)
        low = (head - o * hp) * dh
        sel = ((lane >= low) & (lane < low + dh)).astype(F32).astype(BF16)
        spread = across(ld, sel, 0, 0).astype(BF16)
        at = pl.ds(pl.multiple_of(o * hp * dh, hp * dh), hp * dh)
        dbc[:, at] = jnp.dot(tri, spread, preferred_element_type=F32)
        return carry

    lax.fori_loop(0, zn, decay_cols, 0, unroll=2)

    @pl.when(z == 0)
    def _():
        ch_r[...] = jnp.zeros_like(ch_r)

    pl.semaphore_wait(barrier, (zn - 1) + (group - 1) + (nx - 1))

    def send_e(i, carry):
        to = lax.rem(z + i, zn)
        send(esend, ebuf.at[z], es_sem.at[i], er_sem.at[z], {"inner": to}).start()
        return carry

    lax.fori_loop(1, zn, send_e, 0)

    def chain_copy(h):
        return send(ch_s.at[h], ch_r.at[h], chs_sem.at[h], chr_sem.at[h], {"inner": up_z})

    def chain_head(h):
        @pl.when(z > 0)
        def _():
            chain_copy(h).wait_recv()

        @pl.when(z < zn - 1)
        def _():
            ch_s[h] = (ch_r[h].astype(F32) * factor(0, h) + st[h]).astype(BF16)
            chain_copy(h).start()

    total_steps = heads + STRIDE * (zn - 1)

    def paced(work, first, last):
        def step(n, carry):
            h = n - STRIDE * z

            @pl.when((h >= 0) & (h < heads))
            def _():
                work(h)

            return carry

        first, last = min(first, total_steps), min(last, total_steps)
        if last == first + 1:
            step(first, 0)
        elif last > first:
            lax.fori_loop(first, last, step, 0)

    progress = {"chain": 0, "prior": 0}

    def chain(count):
        paced(chain_head, progress["chain"], progress["chain"] + count)
        progress["chain"] += count

    length = len_ref[0]
    live = (lax.broadcasted_iota(jnp.int32, (rows, 1), 0) + z * rows) < length
    lr = lr_ref[...]
    for load in loads[:3]:
        load.wait()

    def chunk_state(o):
        at = pl.ds(pl.multiple_of(o * hp * dh, hp * dh), hp * dh)
        at_k = pl.ds(pl.multiple_of(wide + o * hp * dh, hp * dh), hp * dh)
        at_v = pl.ds(pl.multiple_of(2 * wide + o * hp * dh, hp * dh), hp * dh)
        kb = jnp.where(live, kv[:, at].astype(F32) + across(lr, up[:, at_k], 0, 0), 0.0)
        vb = jnp.where(live, vv[:, at].astype(F32) + across(lr, up[:, at_v], 0, 0), 0.0)
        kb = kb.astype(BF16)
        vb = vb.astype(BF16)
        kv[:, at] = kb
        vv[:, at] = vb
        d = dbc[:, at]
        scaled = (kb.astype(F32) * jnp.exp(d[rows - 1 :, :] - d)).astype(BF16)
        for k in range(hp):
            span = slice(k * dh, (k + 1) * dh)
            st[o * hp + k] = across(scaled[:, span], vb[:, span], 0, 0)

    pair = 2 if zn % 2 == 0 else 1

    def state_pair(i, carry):
        for j in range(pair):
            chunk_state(pair * i + j)
        if EARLY:
            h = i - STRIDE * z

            @pl.when((h >= 0) & (h < heads))
            def _():
                chain_head(h)

        return carry

    lax.fori_loop(0, zn // pair, state_pair, 0)
    if EARLY:
        progress["chain"] = zn // pair

    def wait_e(i, carry):
        src = lax.rem(z + i, zn)
        send(esend, ebuf.at[src], es_sem.at[i], er_sem.at[src], {"inner": src}).wait_recv()
        return carry

    lax.fori_loop(1, zn, wait_e, 0)
    before = jnp.zeros((1, dh), F32)
    after = jnp.zeros((1, dh), F32)
    whole = jnp.zeros((1, dh), F32)
    for i in range(zn):
        e_i = ebuf[i]
        before = before + jnp.where(z > i, e_i, 0.0)
        after = after + jnp.where(z < i, e_i, 0.0)
        whole = whole + e_i
    keep_exp(1, after)

    def minus_copy(s, k):
        return send(
            ms_s.at[s, k], ms_r.at[s, k], rs_sem.at[s, k], rr_sem.at[s, k], {"inner": down_z}
        )

    def plus_copy(s, k):
        return send(
            ps_s.at[s, k], ps_r.at[s, k], rs_sem.at[rm + s, k], rr_sem.at[rm + s, k],
            {"inner": up_z},
        )

    def reduce_step(copy, out, got, s, o, k):
        h = o * hp + k
        part = st[h] * factor(1, h)
        if s:
            copy(s - 1, k).wait_recv()
            part = part + got[s - 1, k].astype(F32)
        out[s, k] = part.astype(BF16)
        copy(s, k).start()

    for s in range(rm):
        for k in range(hp):
            if s < rp:
                reduce_step(plus_copy, ps_s, ps_r, s, owner_of(rp - s), k)
            reduce_step(minus_copy, ms_s, ms_r, s, owner_of(s - rm), k)
            chain(REDUCE_STEPS[k])
        if s == 0:
            keep_exp(2, before)
            keep_exp(3, whole)

    tile_row = lax.broadcasted_iota(jnp.int32, (slab, dh), 0)
    tile = jnp.zeros((slab, dh), F32)
    for k in range(hp):
        fall = factor(3, z * hp + k)
        high = fall.astype(BF16).astype(F32)
        tile = jnp.where(tile_row == k, high, tile)
        tile = jnp.where(tile_row == k + 4, fall - high, tile)
    parts = []
    for k in range(hp):
        h = z * hp + k
        plus_copy(rp - 1, k).wait_recv()
        minus_copy(rm - 1, k).wait_recv()
        part = st[h] * factor(1, h) + ms_r[rm - 1, k].astype(F32) + ps_r[rp - 1, k].astype(F32)
        parts.append(part.reshape(group, slab, dh))
    parts.append(jnp.broadcast_to(tile[None], (group, slab, dh)))
    c_s[...] = jnp.stack(parts, axis=1).reshape(group, (hp + 1) * slab, dh).astype(BF16)

    def c_copy(peer, slot):
        return send(
            c_s.at[peer], c_r.at[slot], cs_sem.at[peer], cr_sem.at[slot],
            {"ctx": x * group + peer},
        )

    def f_copy(peer, slot):
        return send(
            f_s.at[peer], f_r.at[slot], fs_sem.at[peer], fr_sem.at[slot],
            {"ctx": x * group + peer},
        )

    def x_copy(i, peer, slot):
        return send(
            x_s, x_r.at[slot], xs_sem.at[i], xr_sem.at[slot], {"ctx": peer * group + r}
        )

    def start_c(i, carry):
        c_copy(lax.rem(r + i, group), r).start()
        return carry

    def wait_c(i, carry):
        peer = lax.rem(r + i, group)
        c_copy(peer, peer).wait_recv()
        return carry

    def edit_q(o, carry):
        at = pl.ds(pl.multiple_of(o * hp * dh, hp * dh), hp * dh)
        qv[:, at] = (qv[:, at].astype(F32) + across(lr, up[:, at], 0, 0)).astype(BF16)
        return carry

    def intra(h):
        at = pl.ds(pl.multiple_of(h * dh, dh), dh)
        scores = across(qv[:, at], kv[:, at], 1, 1)
        gap = dbc[:, at][:, 0:rows] - drow[pl.ds(h, 1), :]
        weights = jnp.where(causal, scores * jnp.exp(jnp.where(causal, gap, 0.0)), 0.0)
        oac[:, at] = jnp.dot(weights.astype(BF16), vv[:, at], preferred_element_type=F32)

    units = heads // 2

    def fill(first, last):
        base = progress["chain"] - first

        def unit(u, carry):
            intra(2 * u)
            intra(2 * u + 1)
            h = u + base - STRIDE * z

            @pl.when((h >= 0) & (h < heads))
            def _():
                chain_head(h)

            return carry

        first, last = min(first, units), min(last, units)
        lax.fori_loop(first, last, unit, 0)
        progress["chain"] += last - first

    def prior_term(h):
        at = pl.ds(pl.multiple_of(h * dh, dh), dh)
        inter = jnp.dot(qv[:, at], ch_r[h], preferred_element_type=F32)
        oac[:, at] = oac[:, at] + jnp.exp(dbc[:, at]) * inter

    def prior(count):
        last = min(progress["prior"] + count, progress["chain"])
        paced(prior_term, progress["prior"], last)
        progress["prior"] = last

    lax.fori_loop(1, group, start_c, 0)
    c_r[r] = c_s[r]
    loads[3].wait()
    chain(C_STEPS[0])
    lax.fori_loop(0, zn, edit_q, 0, unroll=2)
    chain(C_STEPS[1])
    fill(0, UNITS[0])
    lax.fori_loop(1, group, wait_c, 0)

    carry_state = [jnp.zeros((slab, dh), F32) for _ in range(hp)]
    carry_decay = [jnp.ones((1, dh), F32) for _ in range(hp)]
    for i in range(group):
        got = c_r[i].astype(F32).reshape(hp + 1, slab, dh)
        for k in range(hp):
            here = got[hp, k : k + 1] + got[hp, k + 4 : k + 5]
            pre[i, k] = carry_state[k]
            cum[i, k] = jnp.broadcast_to(carry_decay[k], (slab, dh))
            carry_state[k] = here * carry_state[k] + got[k]
            carry_decay[k] = here * carry_decay[k]
    tile = jnp.zeros((slab, dh), F32)
    for k in range(hp):
        x_s[k] = carry_state[k]
        tile = jnp.where(tile_row == k, carry_decay[k], tile)
    x_s[hp] = tile

    def start_x(i, carry):
        x_copy(i, lax.rem(x + i, nx), x).start()
        return carry

    def wait_x(i, carry):
        peer = lax.rem(x + i, nx)
        x_copy(i, peer, peer).wait_recv()
        return carry

    lax.fori_loop(1, nx, start_x, 0)
    x_r[x] = x_s[...]
    chain(C_STEPS[2])
    fill(UNITS[0], UNITS[1])
    lax.fori_loop(1, nx, wait_x, 0)
    formers = []
    for k in range(hp):
        entry = jnp.zeros((slab, dh), F32)
        for i in range(nx):
            entry = jnp.where(x > i, x_r[i, hp, k : k + 1] * entry + x_r[i, k], entry)
        formers.append(pre[:, k] + cum[:, k] * entry[None])
    formers.append(jnp.zeros((group, slab, dh), F32))
    f_s[...] = jnp.stack(formers, axis=1).reshape(group, (hp + 1) * slab, dh).astype(BF16)

    def start_f(i, carry):
        f_copy(lax.rem(r + i, group), r).start()
        return carry

    def wait_f(i, carry):
        peer = lax.rem(r + i, group)
        f_copy(peer, peer).wait_recv()
        return carry

    lax.fori_loop(1, group, start_f, 0)
    f_r[r] = f_s[r]
    chain(C_STEPS[3])
    fill(UNITS[1], units)
    prior(P_STEPS)
    lax.fori_loop(1, group, wait_f, 0)
    got = f_r[...].astype(F32).reshape(group, hp + 1, slab, dh)
    for k in range(hp):
        ag[z, k] = got[:, k].reshape(dh, dh).astype(BF16)

    def ag_minus(s, o, k):
        return send(
            ag.at[o, k], ag.at[o, k], as_sem.at[s, k], ar_sem.at[s, k], {"inner": down_z}
        )

    def ag_plus(s, o, k):
        return send(
            ag.at[o, k], ag.at[o, k], as_sem.at[am + s, k], ar_sem.at[am + s, k],
            {"inner": up_z},
        )

    def former_term(o):
        for k in range(hp):
            h = o * hp + k
            at = pl.ds(pl.multiple_of(h * dh, dh), dh)
            inter = jnp.dot(qv[:, at], ag[o, k], preferred_element_type=F32)
            gac[:, at] = jnp.exp(dbc[:, at]) * factor(2, h) * inter

    for k in range(hp):
        ag_plus(0, z, k).start()
        ag_minus(0, z, k).start()
        chain(GATHER_STEPS[k])
    former_term(z)
    rest_p = -(-max(total_steps - progress["prior"], 0) // am)
    final = am - 1
    for s in range(am):
        o_m = owner_of(s + 1)
        o_p = owner_of(-1 - s)
        for k in range(hp):
            if s < ap:
                ag_plus(s, o_p, k).wait_recv()
                if s + 1 < ap:
                    ag_plus(s + 1, o_p, k).start()
            ag_minus(s, o_m, k).wait_recv()
            if s + 1 < am:
                ag_minus(s + 1, o_m, k).start()
            chain(total_steps if s == final and k + 1 == hp else GATHER_STEPS[k])
        if s < ap:
            former_term(o_p)
        former_term(o_m)
        prior(total_steps if s == final else rest_p)

    def mix(h, acc):
        at = pl.ds(pl.multiple_of(h * dh, dh), dh)
        mixed = jnp.where(live, oac[:, at] + gac[:, at], 0.0).astype(BF16)
        qv[:, at] = mixed
        wide_mixed = mixed.astype(F32)
        return acc + wide_mixed * wide_mixed

    acc = lax.fori_loop(0, heads, mix, jnp.zeros((rows, dh), F32), unroll=4)
    mean = jnp.sum(acc, axis=1, keepdims=True) / wide
    inv = lax.rsqrt(mean + 1e-6)

    def scale(h, carry):
        at = pl.ds(pl.multiple_of(h * dh, dh), dh)
        gain = gain_ref[pl.ds(h, 1), :]
        out_ref[:, at] = (qv[:, at].astype(F32) * inv * gain).astype(BF16)
        return carry

    lax.fori_loop(0, heads, scale, 0, unroll=4)

    def left_e(i, carry):
        to = lax.rem(z + i, zn)
        send(esend, ebuf.at[z], es_sem.at[i], er_sem.at[z], {"inner": to}).wait_send()
        return carry

    lax.fori_loop(1, zn, left_e, 0)
    for k in range(hp):
        for s in range(rm):
            minus_copy(s, k).wait_send()
        for s in range(rp):
            plus_copy(s, k).wait_send()
        for s in range(am):
            ag_minus(s, owner_of(s), k).wait_send()
        for s in range(ap):
            ag_plus(s, owner_of(-s), k).wait_send()

    def left_r(i, carry):
        peer = lax.rem(r + i, group)
        c_copy(peer, r).wait_send()
        f_copy(peer, r).wait_send()
        return carry

    lax.fori_loop(1, group, left_r, 0)

    def left_x(i, carry):
        x_copy(i, lax.rem(x + i, nx), x).wait_send()
        return carry

    lax.fori_loop(1, nx, left_x, 0)

    @pl.when(z < zn - 1)
    def _():
        def left_ch(h, carry):
            chain_copy(h).wait_send()
            return carry

        lax.fori_loop(0, heads, left_ch, 0)


def shards(low_rank, q_base, k_base, v_base, edit_up, log_decay, lengths, norm_gain):
    rows, wide = q_base.shape
    rank = low_rank.shape[1]
    heads = log_decay.shape[1]
    dh = wide // heads
    zn = lax.axis_size("inner")
    ctx = lax.axis_size("ctx")
    group = GROUP
    nx = ctx // group
    hp = heads // zn
    rm, rp = split_of(zn, REDUCE_MINUS)
    slab = dh // group
    sizes = (zn, group, nx, heads, hp, rows, dh)
    vmem = pl.BlockSpec(memory_space=pltpu.VMEM)
    anywhere = pl.BlockSpec(memory_space=pl.ANY)
    dma = pltpu.SemaphoreType.DMA
    call = pl.pallas_call(
        functools.partial(kernel, sizes),
        out_shape=jax.ShapeDtypeStruct((rows, wide), BF16),
        in_specs=[
            vmem, anywhere, anywhere, anywhere, anywhere, vmem, vmem,
            pl.BlockSpec(memory_space=pltpu.SMEM),
        ],
        out_specs=vmem,
        scratch_shapes=[
            pltpu.VMEM((rows, wide), BF16),
            pltpu.VMEM((rows, wide), BF16),
            pltpu.VMEM((rows, wide), BF16),
            pltpu.VMEM((rank, 3 * wide), BF16),
            pltpu.VMEM((rows, wide), F32),
            pltpu.VMEM((heads, rows), F32),
            pltpu.VMEM((heads, dh, dh), F32),
            pltpu.VMEM((1, dh), F32),
            pltpu.VMEM((zn, 1, dh), F32),
            pltpu.VMEM((4, dh, dh), F32),
            pltpu.VMEM((rm, hp, dh, dh), BF16),
            pltpu.VMEM((rm, hp, dh, dh), BF16),
            pltpu.VMEM((rp, hp, dh, dh), BF16),
            pltpu.VMEM((rp, hp, dh, dh), BF16),
            pltpu.VMEM((heads, dh, dh), BF16),
            pltpu.VMEM((heads, dh, dh), BF16),
            pltpu.VMEM((group, (hp + 1) * slab, dh), BF16),
            pltpu.VMEM((group, (hp + 1) * slab, dh), BF16),
            pltpu.VMEM((group, hp, slab, dh), F32),
            pltpu.VMEM((group, hp, slab, dh), F32),
            pltpu.VMEM((group, (hp + 1) * slab, dh), BF16),
            pltpu.VMEM((group, (hp + 1) * slab, dh), BF16),
            pltpu.VMEM((hp + 1, slab, dh), F32),
            pltpu.VMEM((nx, hp + 1, slab, dh), F32),
            pltpu.VMEM((zn, hp, dh, dh), BF16),
            pltpu.VMEM((rows, wide), F32),
            pltpu.VMEM((rows, wide), F32),
            dma((4,)),
            dma((zn,)), dma((zn,)),
            dma((zn - 1, hp)), dma((zn - 1, hp)),
            dma((heads,)), dma((heads,)),
            dma((group,)), dma((group,)),
            dma((group,)), dma((group,)),
            dma((nx,)), dma((nx,)),
            dma((zn - 1, hp)), dma((zn - 1, hp)),
        ],
        compiler_params=pltpu.CompilerParams(
            collective_id=0, has_side_effects=True, vmem_limit_bytes=60 * 1024 * 1024
        ),
    )
    return call(
        low_rank.T, q_base, k_base, v_base, edit_up, log_decay.T,
        norm_gain.reshape(heads, dh), lengths,
    )


def solution(mesh):
    rows = P(("ctx", "inner"), None)
    return jax.shard_map(
        shards,
        mesh=mesh,
        in_specs=(rows, rows, rows, rows, P(), rows, P("ctx"), P()),
        out_specs=rows,
        check_vma=False,
    )
```

```python
import functools

import jax
import jax.numpy as jnp
from jax import lax
from jax.experimental import pallas as pl
from jax.experimental.pallas import tpu as pltpu
from jax.sharding import PartitionSpec as P

MESH = pl.DeviceIdType.MESH
F32 = jnp.float32
BF16 = jnp.bfloat16
GROUP = 16
STRIDE = 4
EARLY = True
REDUCE_MINUS = 6
GATHER_MINUS = 6
REDUCE_STEPS = (1, 1, 1)
GATHER_STEPS = (1, 2, 1)
UNITS = (8, 11)
C_STEPS = (1, 1, 1, 1)
P_STEPS = 24


def split_of(zn, minus):
    minus = min(max(minus, zn // 2), zn - 2)
    return minus, zn - 1 - minus


def across(a, b, left, right):
    return lax.dot_general(a, b, (((left,), (right,)), ((), ())), preferred_element_type=F32)


def kernel(
    sizes,
    lr_ref, q_hbm, k_hbm, v_hbm, up_hbm, ld_ref, gain_ref, len_ref,
    out_ref,
    qv, kv, vv, up, dbc, drow, st, esend, ebuf, cols,
    ms_s, ms_r, ps_s, ps_r, ch_s, ch_r,
    c_s, c_r, pre, cum, f_s, f_r, x_s, x_r, ag, oac, gac,
    in_sem, es_sem, er_sem, rs_sem, rr_sem, chs_sem, chr_sem,
    cs_sem, cr_sem, fs_sem, fr_sem, xs_sem, xr_sem, as_sem, ar_sem,
):
    zn, group, nx, heads, hp, rows, dh = sizes
    rm, rp = split_of(zn, REDUCE_MINUS)
    am, ap = split_of(zn, GATHER_MINUS)
    wide = heads * dh
    slab = dh // group
    z = lax.axis_index("inner")
    c = lax.axis_index("ctx")
    r = lax.rem(c, group)
    x = c // group
    up_z = lax.rem(z + 1, zn)
    down_z = lax.rem(z + zn - 1, zn)

    def owner_of(shift):
        return lax.rem(z + shift + zn, zn)

    def send(src, dst, s_sem, r_sem, where):
        copy = pltpu.make_async_remote_copy(
            src_ref=src, dst_ref=dst, send_sem=s_sem, recv_sem=r_sem,
            device_id=where, device_id_type=MESH,
        )
        return copy

    loads = [
        pltpu.make_async_copy(src, dst, in_sem.at[i])
        for i, (src, dst) in enumerate(((k_hbm, kv), (v_hbm, vv), (up_hbm, up), (q_hbm, qv)))
    ]
    for load in loads:
        load.start()

    barrier = pltpu.get_barrier_semaphore()

    def greet_z(i, carry):
        pl.semaphore_signal(
            barrier, inc=1, device_id={"inner": lax.rem(z + i, zn)}, device_id_type=MESH
        )
        return carry

    def greet_r(i, carry):
        pl.semaphore_signal(
            barrier, inc=1, device_id={"ctx": x * group + lax.rem(r + i, group)},
            device_id_type=MESH,
        )
        return carry

    def greet_x(i, carry):
        pl.semaphore_signal(
            barrier, inc=1, device_id={"ctx": lax.rem(x + i, nx) * group + r},
            device_id_type=MESH,
        )
        return carry

    lax.fori_loop(1, zn, greet_z, 0)
    lax.fori_loop(1, group, greet_r, 0)
    lax.fori_loop(1, nx, greet_x, 0)

    ld = ld_ref[...]
    row_i = lax.broadcasted_iota(jnp.int32, (rows, rows), 0)
    col_i = lax.broadcasted_iota(jnp.int32, (rows, rows), 1)
    causal = row_i >= col_i
    tri = causal.astype(F32).astype(BF16)
    triu = (row_i <= col_i).astype(F32).astype(BF16)
    drow[...] = jnp.dot(ld, triu, preferred_element_type=F32)
    lane_head = lax.broadcasted_iota(jnp.int32, (heads, dh), 1)
    pick = (lane_head == lax.broadcasted_iota(jnp.int32, (heads, dh), 0)).astype(F32).astype(BF16)
    per_head = across(ld, pick, 0, 0).astype(BF16)
    esend[...] = jnp.dot(jnp.ones((8, rows), BF16), per_head, preferred_element_type=F32)[0:1]
    ebuf[z] = esend[...]
    eye = lax.broadcasted_iota(jnp.int32, (dh, dh), 0) == lax.broadcasted_iota(
        jnp.int32, (dh, dh), 1
    )

    def keep_exp(kind, vec):
        column = jnp.sum(jnp.where(eye, vec, 0.0), axis=1, keepdims=True)
        cols[kind] = jnp.broadcast_to(jnp.exp(column), (dh, dh))

    def factor(kind, head):
        return cols[kind, pl.ds(head, 1), :]

    keep_exp(0, esend[...])

    def decay_cols(o, carry):
        lane = lax.broadcasted_iota(jnp.int32, (heads, hp * dh), 1)
        head = lax.broadcasted_iota(jnp.int32, (heads, hp * dh), 0)
        low = (head - o * hp) * dh
        sel = ((lane >= low) & (lane < low + dh)).astype(F32).astype(BF16)
        spread = across(ld, sel, 0, 0).astype(BF16)
        at = pl.ds(pl.multiple_of(o * hp * dh, hp * dh), hp * dh)
        dbc[:, at] = jnp.dot(tri, spread, preferred_element_type=F32)
        return carry

    lax.fori_loop(0, zn, decay_cols, 0, unroll=2)

    @pl.when(z == 0)
    def _():
        ch_r[...] = jnp.zeros_like(ch_r)

    pl.semaphore_wait(barrier, (zn - 1) + (group - 1) + (nx - 1))

    def send_e(i, carry):
        to = lax.rem(z + i, zn)
        send(esend, ebuf.at[z], es_sem.at[i], er_sem.at[z], {"inner": to}).start()
        return carry

    lax.fori_loop(1, zn, send_e, 0)

    def chain_copy(h):
        return send(ch_s.at[h], ch_r.at[h], chs_sem.at[h], chr_sem.at[h], {"inner": up_z})

    def chain_head(h):
        @pl.when(z > 0)
        def _():
            chain_copy(h).wait_recv()

        @pl.when(z < zn - 1)
        def _():
            ch_s[h] = (ch_r[h].astype(F32) * factor(0, h) + st[h]).astype(BF16)
            chain_copy(h).start()

    total_steps = heads + STRIDE * (zn - 1)

    def paced(work, first, last):
        def step(n, carry):
            h = n - STRIDE * z

            @pl.when((h >= 0) & (h < heads))
            def _():
                work(h)

            return carry

        first, last = min(first, total_steps), min(last, total_steps)
        if last == first + 1:
            step(first, 0)
        elif last > first:
            lax.fori_loop(first, last, step, 0)

    progress = {"chain": 0, "prior": 0}

    def chain(count):
        paced(chain_head, progress["chain"], progress["chain"] + count)
        progress["chain"] += count

    length = len_ref[0]
    live = (lax.broadcasted_iota(jnp.int32, (rows, 1), 0) + z * rows) < length
    lr = lr_ref[...]
    for load in loads[:3]:
        load.wait()

    def chunk_state(o):
        at = pl.ds(pl.multiple_of(o * hp * dh, hp * dh), hp * dh)
        at_k = pl.ds(pl.multiple_of(wide + o * hp * dh, hp * dh), hp * dh)
        at_v = pl.ds(pl.multiple_of(2 * wide + o * hp * dh, hp * dh), hp * dh)
        kb = jnp.where(live, kv[:, at].astype(F32) + across(lr, up[:, at_k], 0, 0), 0.0)
        vb = jnp.where(live, vv[:, at].astype(F32) + across(lr, up[:, at_v], 0, 0), 0.0)
        kb = kb.astype(BF16)
        vb = vb.astype(BF16)
        kv[:, at] = kb
        vv[:, at] = vb
        d = dbc[:, at]
        scaled = (kb.astype(F32) * jnp.exp(d[rows - 1 :, :] - d)).astype(BF16)
        for k in range(hp):
            span = slice(k * dh, (k + 1) * dh)
            st[o * hp + k] = across(scaled[:, span], vb[:, span], 0, 0)

    pair = 2 if zn % 2 == 0 else 1

    def state_pair(i, carry):
        for j in range(pair):
            chunk_state(pair * i + j)
        if EARLY:
            h = i - STRIDE * z

            @pl.when((h >= 0) & (h < heads))
            def _():
                chain_head(h)

        return carry

    lax.fori_loop(0, zn // pair, state_pair, 0)
    if EARLY:
        progress["chain"] = zn // pair

    def wait_e(i, carry):
        src = lax.rem(z + i, zn)
        send(esend, ebuf.at[src], es_sem.at[i], er_sem.at[src], {"inner": src}).wait_recv()
        return carry

    lax.fori_loop(1, zn, wait_e, 0)
    before = jnp.zeros((1, dh), F32)
    after = jnp.zeros((1, dh), F32)
    whole = jnp.zeros((1, dh), F32)
    for i in range(zn):
        e_i = ebuf[i]
        before = before + jnp.where(z > i, e_i, 0.0)
        after = after + jnp.where(z < i, e_i, 0.0)
        whole = whole + e_i
    keep_exp(1, after)

    def minus_copy(s, k):
        return send(
            ms_s.at[s, k], ms_r.at[s, k], rs_sem.at[s, k], rr_sem.at[s, k], {"inner": down_z}
        )

    def plus_copy(s, k):
        return send(
            ps_s.at[s, k], ps_r.at[s, k], rs_sem.at[rm + s, k], rr_sem.at[rm + s, k],
            {"inner": up_z},
        )

    def reduce_step(copy, out, got, s, o, k):
        h = o * hp + k
        part = st[h] * factor(1, h)
        if s:
            copy(s - 1, k).wait_recv()
            part = part + got[s - 1, k].astype(F32)
        out[s, k] = part.astype(BF16)
        copy(s, k).start()

    for s in range(rm):
        for k in range(hp):
            reduce_step(minus_copy, ms_s, ms_r, s, owner_of(s - rm), k)
            if s < rp:
                reduce_step(plus_copy, ps_s, ps_r, s, owner_of(rp - s), k)
            chain(REDUCE_STEPS[k])
        if s == 0:
            keep_exp(2, before)
            keep_exp(3, whole)

    tile_row = lax.broadcasted_iota(jnp.int32, (slab, dh), 0)
    tile = jnp.zeros((slab, dh), F32)
    for k in range(hp):
        fall = factor(3, z * hp + k)
        high = fall.astype(BF16).astype(F32)
        tile = jnp.where(tile_row == k, high, tile)
        tile = jnp.where(tile_row == k + 4, fall - high, tile)
    parts = []
    for k in range(hp):
        h = z * hp + k
        plus_copy(rp - 1, k).wait_recv()
        minus_copy(rm - 1, k).wait_recv()
        part = st[h] * factor(1, h) + ms_r[rm - 1, k].astype(F32) + ps_r[rp - 1, k].astype(F32)
        parts.append(part.reshape(group, slab, dh))
    parts.append(jnp.broadcast_to(tile[None], (group, slab, dh)))
    c_s[...] = jnp.stack(parts, axis=1).reshape(group, (hp + 1) * slab, dh).astype(BF16)

    def c_copy(peer, slot):
        return send(
            c_s.at[peer], c_r.at[slot], cs_sem.at[peer], cr_sem.at[slot],
            {"ctx": x * group + peer},
        )

    def f_copy(peer, slot):
        return send(
            f_s.at[peer], f_r.at[slot], fs_sem.at[peer], fr_sem.at[slot],
            {"ctx": x * group + peer},
        )

    def x_copy(i, peer, slot):
        return send(
            x_s, x_r.at[slot], xs_sem.at[i], xr_sem.at[slot], {"ctx": peer * group + r}
        )

    def start_c(i, carry):
        c_copy(lax.rem(r + i, group), r).start()
        return carry

    def wait_c(i, carry):
        peer = lax.rem(r + i, group)
        c_copy(peer, peer).wait_recv()
        return carry

    def edit_q(o, carry):
        at = pl.ds(pl.multiple_of(o * hp * dh, hp * dh), hp * dh)
        qv[:, at] = (qv[:, at].astype(F32) + across(lr, up[:, at], 0, 0)).astype(BF16)
        return carry

    def intra(h):
        at = pl.ds(pl.multiple_of(h * dh, dh), dh)
        scores = across(qv[:, at], kv[:, at], 1, 1)
        gap = dbc[:, at][:, 0:rows] - drow[pl.ds(h, 1), :]
        weights = jnp.where(causal, scores * jnp.exp(jnp.where(causal, gap, 0.0)), 0.0)
        oac[:, at] = jnp.dot(weights.astype(BF16), vv[:, at], preferred_element_type=F32)

    units = heads // 2

    def fill(first, last):
        base = progress["chain"] - first

        def unit(u, carry):
            intra(2 * u)
            intra(2 * u + 1)
            h = u + base - STRIDE * z

            @pl.when((h >= 0) & (h < heads))
            def _():
                chain_head(h)

            return carry

        first, last = min(first, units), min(last, units)
        lax.fori_loop(first, last, unit, 0)
        progress["chain"] += last - first

    def prior_term(h):
        at = pl.ds(pl.multiple_of(h * dh, dh), dh)
        inter = jnp.dot(qv[:, at], ch_r[h], preferred_element_type=F32)
        oac[:, at] = oac[:, at] + jnp.exp(dbc[:, at]) * inter

    def prior(count):
        last = min(progress["prior"] + count, progress["chain"])
        paced(prior_term, progress["prior"], last)
        progress["prior"] = last

    lax.fori_loop(1, group, start_c, 0)
    c_r[r] = c_s[r]
    loads[3].wait()
    chain(C_STEPS[0])
    lax.fori_loop(0, zn, edit_q, 0, unroll=2)
    chain(C_STEPS[1])
    fill(0, UNITS[0])
    lax.fori_loop(1, group, wait_c, 0)

    carry_state = [jnp.zeros((slab, dh), F32) for _ in range(hp)]
    carry_decay = [jnp.ones((1, dh), F32) for _ in range(hp)]
    for i in range(group):
        got = c_r[i].astype(F32).reshape(hp + 1, slab, dh)
        for k in range(hp):
            here = got[hp, k : k + 1] + got[hp, k + 4 : k + 5]
            pre[i, k] = carry_state[k]
            cum[i, k] = jnp.broadcast_to(carry_decay[k], (slab, dh))
            carry_state[k] = here * carry_state[k] + got[k]
            carry_decay[k] = here * carry_decay[k]
    tile = jnp.zeros((slab, dh), F32)
    for k in range(hp):
        x_s[k] = carry_state[k]
        tile = jnp.where(tile_row == k, carry_decay[k], tile)
    x_s[hp] = tile

    def start_x(i, carry):
        x_copy(i, lax.rem(x + i, nx), x).start()
        return carry

    def wait_x(i, carry):
        peer = lax.rem(x + i, nx)
        x_copy(i, peer, peer).wait_recv()
        return carry

    lax.fori_loop(1, nx, start_x, 0)
    x_r[x] = x_s[...]
    chain(C_STEPS[2])
    fill(UNITS[0], UNITS[1])
    lax.fori_loop(1, nx, wait_x, 0)
    formers = []
    for k in range(hp):
        entry = jnp.zeros((slab, dh), F32)
        for i in range(nx):
            entry = jnp.where(x > i, x_r[i, hp, k : k + 1] * entry + x_r[i, k], entry)
        formers.append(pre[:, k] + cum[:, k] * entry[None])
    formers.append(jnp.zeros((group, slab, dh), F32))
    f_s[...] = jnp.stack(formers, axis=1).reshape(group, (hp + 1) * slab, dh).astype(BF16)

    def start_f(i, carry):
        f_copy(lax.rem(r + i, group), r).start()
        return carry

    def wait_f(i, carry):
        peer = lax.rem(r + i, group)
        f_copy(peer, peer).wait_recv()
        return carry

    lax.fori_loop(1, group, start_f, 0)
    f_r[r] = f_s[r]
    chain(C_STEPS[3])
    fill(UNITS[1], units)
    prior(P_STEPS)
    lax.fori_loop(1, group, wait_f, 0)
    got = f_r[...].astype(F32).reshape(group, hp + 1, slab, dh)
    for k in range(hp):
        ag[z, k] = got[:, k].reshape(dh, dh).astype(BF16)

    def ag_minus(s, o, k):
        return send(
            ag.at[o, k], ag.at[o, k], as_sem.at[s, k], ar_sem.at[s, k], {"inner": down_z}
        )

    def ag_plus(s, o, k):
        return send(
            ag.at[o, k], ag.at[o, k], as_sem.at[am + s, k], ar_sem.at[am + s, k],
            {"inner": up_z},
        )

    def former_term(o):
        for k in range(hp):
            h = o * hp + k
            at = pl.ds(pl.multiple_of(h * dh, dh), dh)
            inter = jnp.dot(qv[:, at], ag[o, k], preferred_element_type=F32)
            gac[:, at] = jnp.exp(dbc[:, at]) * factor(2, h) * inter

    for k in range(hp):
        ag_minus(0, z, k).start()
        ag_plus(0, z, k).start()
        chain(GATHER_STEPS[k])
    former_term(z)
    rest_p = -(-max(total_steps - progress["prior"], 0) // am)
    final = am - 1
    for s in range(am):
        o_m = owner_of(s + 1)
        o_p = owner_of(-1 - s)
        for k in range(hp):
            ag_minus(s, o_m, k).wait_recv()
            if s + 1 < am:
                ag_minus(s + 1, o_m, k).start()
            if s < ap:
                ag_plus(s, o_p, k).wait_recv()
                if s + 1 < ap:
                    ag_plus(s + 1, o_p, k).start()
            chain(total_steps if s == final and k + 1 == hp else GATHER_STEPS[k])
        if s < ap:
            former_term(o_p)
        former_term(o_m)
        prior(total_steps if s == final else rest_p)

    def mix(h, acc):
        at = pl.ds(pl.multiple_of(h * dh, dh), dh)
        mixed = jnp.where(live, oac[:, at] + gac[:, at], 0.0).astype(BF16)
        qv[:, at] = mixed
        wide_mixed = mixed.astype(F32)
        return acc + wide_mixed * wide_mixed

    acc = lax.fori_loop(0, heads, mix, jnp.zeros((rows, dh), F32), unroll=4)
    mean = jnp.sum(acc, axis=1, keepdims=True) / wide
    inv = lax.rsqrt(mean + 1e-6)

    def scale(h, carry):
        at = pl.ds(pl.multiple_of(h * dh, dh), dh)
        gain = gain_ref[pl.ds(h, 1), :]
        out_ref[:, at] = (qv[:, at].astype(F32) * inv * gain).astype(BF16)
        return carry

    lax.fori_loop(0, heads, scale, 0, unroll=4)

    def left_e(i, carry):
        to = lax.rem(z + i, zn)
        send(esend, ebuf.at[z], es_sem.at[i], er_sem.at[z], {"inner": to}).wait_send()
        return carry

    lax.fori_loop(1, zn, left_e, 0)
    for k in range(hp):
        for s in range(rm):
            minus_copy(s, k).wait_send()
        for s in range(rp):
            plus_copy(s, k).wait_send()
        for s in range(am):
            ag_minus(s, owner_of(s), k).wait_send()
        for s in range(ap):
            ag_plus(s, owner_of(-s), k).wait_send()

    def left_r(i, carry):
        peer = lax.rem(r + i, group)
        c_copy(peer, r).wait_send()
        f_copy(peer, r).wait_send()
        return carry

    lax.fori_loop(1, group, left_r, 0)

    def left_x(i, carry):
        x_copy(i, lax.rem(x + i, nx), x).wait_send()
        return carry

    lax.fori_loop(1, nx, left_x, 0)

    @pl.when(z < zn - 1)
    def _():
        def left_ch(h, carry):
            chain_copy(h).wait_send()
            return carry

        lax.fori_loop(0, heads, left_ch, 0)


def shards(low_rank, q_base, k_base, v_base, edit_up, log_decay, lengths, norm_gain):
    rows, wide = q_base.shape
    rank = low_rank.shape[1]
    heads = log_decay.shape[1]
    dh = wide // heads
    zn = lax.axis_size("inner")
    ctx = lax.axis_size("ctx")
    group = GROUP
    nx = ctx // group
    hp = heads // zn
    rm, rp = split_of(zn, REDUCE_MINUS)
    slab = dh // group
    sizes = (zn, group, nx, heads, hp, rows, dh)
    vmem = pl.BlockSpec(memory_space=pltpu.VMEM)
    anywhere = pl.BlockSpec(memory_space=pl.ANY)
    dma = pltpu.SemaphoreType.DMA
    call = pl.pallas_call(
        functools.partial(kernel, sizes),
        out_shape=jax.ShapeDtypeStruct((rows, wide), BF16),
        in_specs=[
            vmem, anywhere, anywhere, anywhere, anywhere, vmem, vmem,
            pl.BlockSpec(memory_space=pltpu.SMEM),
        ],
        out_specs=vmem,
        scratch_shapes=[
            pltpu.VMEM((rows, wide), BF16),
            pltpu.VMEM((rows, wide), BF16),
            pltpu.VMEM((rows, wide), BF16),
            pltpu.VMEM((rank, 3 * wide), BF16),
            pltpu.VMEM((rows, wide), F32),
            pltpu.VMEM((heads, rows), F32),
            pltpu.VMEM((heads, dh, dh), F32),
            pltpu.VMEM((1, dh), F32),
            pltpu.VMEM((zn, 1, dh), F32),
            pltpu.VMEM((4, dh, dh), F32),
            pltpu.VMEM((rm, hp, dh, dh), BF16),
            pltpu.VMEM((rm, hp, dh, dh), BF16),
            pltpu.VMEM((rp, hp, dh, dh), BF16),
            pltpu.VMEM((rp, hp, dh, dh), BF16),
            pltpu.VMEM((heads, dh, dh), BF16),
            pltpu.VMEM((heads, dh, dh), BF16),
            pltpu.VMEM((group, (hp + 1) * slab, dh), BF16),
            pltpu.VMEM((group, (hp + 1) * slab, dh), BF16),
            pltpu.VMEM((group, hp, slab, dh), F32),
            pltpu.VMEM((group, hp, slab, dh), F32),
            pltpu.VMEM((group, (hp + 1) * slab, dh), BF16),
            pltpu.VMEM((group, (hp + 1) * slab, dh), BF16),
            pltpu.VMEM((hp + 1, slab, dh), F32),
            pltpu.VMEM((nx, hp + 1, slab, dh), F32),
            pltpu.VMEM((zn, hp, dh, dh), BF16),
            pltpu.VMEM((rows, wide), F32),
            pltpu.VMEM((rows, wide), F32),
            dma((4,)),
            dma((zn,)), dma((zn,)),
            dma((zn - 1, hp)), dma((zn - 1, hp)),
            dma((heads,)), dma((heads,)),
            dma((group,)), dma((group,)),
            dma((group,)), dma((group,)),
            dma((nx,)), dma((nx,)),
            dma((zn - 1, hp)), dma((zn - 1, hp)),
        ],
        compiler_params=pltpu.CompilerParams(
            collective_id=0, has_side_effects=True, vmem_limit_bytes=60 * 1024 * 1024
        ),
    )
    return call(
        low_rank.T, q_base, k_base, v_base, edit_up, log_decay.T,
        norm_gain.reshape(heads, dh), lengths,
    )


def solution(mesh):
    rows = P(("ctx", "inner"), None)
    return jax.shard_map(
        shards,
        mesh=mesh,
        in_specs=(rows, rows, rows, rows, P(), rows, P("ctx"), P()),
        out_specs=rows,
        check_vma=False,
    )
```
